256 devices in a mesh: rows: 16 (over y, x_hi, core), chan: 16 (over x_lo, z).
Axes of the slice: x: 4 (x_hi: 2, x_lo: 2; x = x_hi * 2 + x_lo), y: 4, z: 8, core: 2. Of those that a mesh axis runs over, the one named last changes fastest.
Arguments:
- features: bfloat16 [1024, 1, 8192], P('chan', None, 'rows'), may hold values from -24 to 24
- gain_first: float32 [1024], P('chan'), may hold values from 0.1 to 1.9
- weight_first: bfloat16 [3, 3, 3, 1024, 1024], P(None, None, None, 'chan'), may hold values from -0.0390625 to 0.0390625
- bias_first: float32 [1024], P('chan'), may hold values from -3 to 3
- gain_second: float32 [1024], P('chan'), may hold values from 0.1 to 1.9
- weight_second: bfloat16 [3, 3, 3, 1024, 1024], P(None, None, None, 'chan'), may hold values from -0.0390625 to 0.0390625
- bias_second: float32 [1024], P('chan'), may hold values from -3 to 3
Outputs:
- block_out: bfloat16 [1024, 1, 8192], P('chan', None, 'rows')
The draws below stay inside these ranges and needn't reach their ends.
All inputs are finite; a program needn't handle non-finite values.
Results may differ from the reference program's by a relative error of at most 0.0022.
Values may be sent and summed in bfloat16 or wider, within the bound.
A program may use at most 64 MiB of HBM per device.

```python
import jax
import jax.numpy as jnp
from jax import lax

CH = 1024
FRAMES = 1
WIDTH = 64
HEIGHT = 128


def draw_features(key, part):
    first_key, second_key = jax.random.split(jax.random.fold_in(key, 11), 2)
    channel_scale = jnp.exp(jnp.log(3.0) * jnp.arange(CH, dtype=jnp.float32) / CH)[:, None, None]
    cell_scale = jnp.exp(jax.random.uniform(second_key, (1, FRAMES, HEIGHT * WIDTH), jnp.float32, -0.69, 0.69))
    base = jnp.clip(jax.random.normal(first_key, (CH, FRAMES, HEIGHT * WIDTH), jnp.float32), -4.0, 4.0)
    return (base * channel_scale * cell_scale).astype(jnp.bfloat16)


def steps_of(rng, extent, shards, smallest, high):
    level = 1.0
    for dim, blocks in shards:
        draws = jax.random.uniform(jax.random.fold_in(jax.random.fold_in(rng, 6), dim), (blocks,), jnp.float32, smallest / len(shards), high / len(shards))
        level = level * jnp.repeat(jnp.exp(draws), extent[dim] // blocks).reshape((-1,) + (1,) * (len(extent) - 1 - dim))
    return level


def centred(key, dims, deviation, limit, cuts=(), kind=jnp.bfloat16):
    level = steps_of(key, dims, cuts, -0.22, 0.18) if cuts else 1.0
    entries = jax.random.normal(key, dims, jnp.float32) * deviation * level
    return jnp.minimum(jnp.maximum(entries, -limit), limit).astype(kind)


def setup_inputs(seed: int = 0) -> dict:
    splits = jax.random.split(jax.random.key(seed), 8)
    return {
        "features": draw_features(jax.random.fold_in(splits[7], 71), 0),
        "gain_first": jnp.clip(1.0 + 0.18 * jax.random.normal(splits[1], (CH,), jnp.float32), 0.1, 1.9),
        "weight_first": centred(splits[2], (3, 3, 3, CH, CH), (27 * CH) ** -0.5, 0.0390625, ((3, 16),)),
        "bias_first": centred(splits[3], (CH,), 0.5, 3.0, ((0, 16),), jnp.float32),
        "gain_second": jnp.clip(1.0 + 0.18 * jax.random.normal(splits[4], (CH,), jnp.float32), 0.1, 1.9),
        "weight_second": centred(splits[5], (3, 3, 3, CH, CH), (27 * CH) ** -0.5, 0.0390625, ((3, 16),)),
        "bias_second": centred(splits[6], (CH,), 0.5, 3.0, ((0, 16),), jnp.float32),
    }


def activate(values, gain):
    mean_sq = lax.optimization_barrier(jnp.mean(values * values, axis=0, keepdims=True))
    return jax.nn.silu(values * gain[:, None, None] / jnp.sqrt(mean_sq + 1e-06)).astype(jnp.bfloat16)

def convolve(data, kernel):
    channels, frames, cells = data.shape
    grid = data.reshape(1, channels, frames, HEIGHT, WIDTH)
    result = lax.conv_general_dilated(grid, kernel, (1, 1, 1), ((2, 0), (1, 1), (1, 1)), dimension_numbers=('NCDHW', 'DHWOI', 'NCDHW'), preferred_element_type=jnp.float32)
    return result[0].astype(jnp.float32).reshape(kernel.shape[3], frames, cells)

def reference(features, gain_first, weight_first, bias_first, gain_second, weight_second, bias_second):
    source = features.astype(jnp.float32)
    first = activate(source, gain_first)
    middle = convolve(first, weight_first) + bias_first[:, None, None]
    second = activate(middle, gain_second)
    return (source + convolve(second, weight_second) + bias_second[:, None, None]).astype(jnp.bfloat16)
```

```python
import jax
import jax.numpy as jnp
from jax import lax
from jax.experimental import pallas as pl
from jax.experimental.pallas import tpu as pltpu
from jax.sharding import PartitionSpec as P

CH = 1024
WIDTH = 64
EPS = 1e-6
F32 = jnp.float32
BF16 = jnp.bfloat16
MESH = pl.DeviceIdType.MESH

OUTER, INNER = 0, 1
PART = {"a": slice(0, 32), "b": slice(32, 64)}


def last_step(half, kind, d):
    if kind == "t":
        far = d > 0
    elif kind == "a0":
        far = d > 0
    elif kind == "a1":
        far = d < 0
    else:
        far = (d > 0) == (half == OUTER)
    return 4 if far else 3


def item_keys():
    keys = [("t", None, 1, 0)]
    for d in (1, -1):
        keys += [("t", None, d, k) for k in range(1, last_step(None, "t", d) + 1)]
    for half in (OUTER, INNER):
        keys += [("a1", half, 1, 0), ("b1", half, 1, 0)]
        for d in (1, -1):
            for kind in ("a0", "a1", "b0"):
                keys += [(kind, half, d, k) for k in range(1, last_step(half, kind, d) + 1)]
            keys += [("b1", half, d, k) for k in range(1, last_step(half, "b0", d) + 1)]
    return keys


KEYS = item_keys()
INDEX = {key: i for i, key in enumerate(KEYS)}


class Gather:
    def __init__(self, x, z, blocks, tiles, send_sem, recv_sem):
        self.x, self.z = x, z
        self.blocks, self.tiles = blocks, tiles
        self.send_sem, self.recv_sem = send_sem, recv_sem
        self.sent = []

    def ref(self, key):
        kind, half, d, k = key
        source = lax.rem(self.z - d * k + 8, 8)
        if kind == "t":
            return self.tiles.at[source] if k else self.tiles.at[source, 1 - self.x]
        column = self.x if kind.endswith("0") else 1 - self.x
        return self.blocks[half].at[column * 8 + source, PART[kind[0]]]

    def copy(self, src, key, chan):
        i = INDEX[key]
        return pltpu.make_async_remote_copy(
            src_ref=src,
            dst_ref=src,
            send_sem=self.send_sem.at[i],
            recv_sem=self.recv_sem.at[i],
            device_id={"chan": chan},
            device_id_type=MESH,
        )

    def send(self, src, key, chan):
        copy = self.copy(src, key, chan)
        copy.start()
        self.sent.append(copy)

    def along(self, d):
        return self.x * 8 + lax.rem(self.z + d + 8, 8)

    def across(self):
        return (1 - self.x) * 8 + self.z

    def own(self, half, part):
        return self.blocks[half].at[self.x * 8 + self.z, PART[part]]

    def wait(self, key):
        self.copy(self.ref(key), key, self.across()).wait_recv()

    def start_blocks(self, half):
        self.send(self.own(half, "a"), ("a1", half, 1, 0), self.across())
        for d in (1, -1):
            self.send(self.own(half, "b"), ("b0", half, d, 1), self.along(d))
        for d in (1, -1):
            self.send(self.own(half, "a"), ("a0", half, d, 1), self.along(d))
        self.send(self.own(half, "b"), ("b1", half, 1, 0), self.across())

    def start_tile(self):
        self.send(self.tiles.at[self.z, self.x], ("t", None, 1, 0), self.across())

    def relay_tile(self, k):
        for d in (1, -1):
            if k > last_step(None, "t", d):
                continue
            if k or d > 0:
                self.wait(("t", None, d, k))
            if k < last_step(None, "t", d):
                src = self.tiles.at[lax.rem(self.z - d * k + 8, 8)]
                self.send(src, ("t", None, d, k + 1), self.along(d))

    def relay_blocks(self, half, k):
        kinds = ("b0", "a0", "a1") if k else ("a1",)
        for kind in kinds:
            for d in (1, -1):
                if k > last_step(half, kind, d):
                    continue
                key = (kind, half, d, k)
                if k or d > 0:
                    self.wait(key)
                src = self.ref(key)
                if k < last_step(half, kind, d):
                    self.send(src, (kind, half, d, k + 1), self.along(d))
                if kind == "b0":
                    self.send(src, ("b1", half, d, k), self.across())

    def finish_blocks(self, half):
        self.wait(("b1", half, 1, 0))
        for k in range(1, 5):
            for d in (1, -1):
                if k <= last_step(half, "b0", d):
                    self.wait(("b1", half, d, k))

    def wait_sends(self):
        for copy in self.sent:
            copy.wait_send()


def silu_of_half(h):
    return h * (1.0 + jnp.tanh(h))


def scale_rows(tiles, factor):
    total = jnp.sum(tiles[:, :, 0:4, :], axis=(0, 1))
    return lax.rsqrt(total / CH + EPS) * factor


def kernel(
    feat, g1, w1, b1, g2, w2, b2, out,
    x_out, x_in, m_out, m_in, t1, t2, act, wa, wb, y, rows, halo_src, halo_dst,
    load_sem, send1, recv1, send2, recv2, halo_send, halo_recv,
):
    r, c = lax.axis_index("rows"), lax.axis_index("chan")
    x, z = c // 8, lax.rem(c, 8)
    above, below = lax.rem(r + 15, 16), lax.rem(r + 1, 16)

    loads = [
        pltpu.make_async_copy(feat.at[:, 0:128], x_out.at[c, :, 0:128], load_sem.at[0]),
        pltpu.make_async_copy(feat.at[:, 384:512], x_out.at[c, :, 128:256], load_sem.at[1]),
        pltpu.make_async_copy(feat.at[:, 128:384], x_in.at[c], load_sem.at[2]),
        pltpu.make_async_copy(w1.at[pl.ds(18 * 64, 9 * 64)], wa, load_sem.at[3]),
        pltpu.make_async_copy(w2.at[pl.ds(18 * 64, 9 * 64)], wb, load_sem.at[4]),
    ]
    for load in loads:
        load.start()

    barrier = pltpu.get_barrier_semaphore()
    for chan in (x * 8 + lax.rem(z + 1, 8), x * 8 + lax.rem(z + 7, 8), (1 - x) * 8 + z):
        pl.semaphore_signal(barrier, inc=1, device_id={"chan": chan}, device_id_type=MESH)
    for row in (above, below):
        pl.semaphore_signal(barrier, inc=1, device_id={"rows": row}, device_id_type=MESH)
    rows[...] = jnp.zeros_like(rows)
    rows[0:1, 0:64] = g2[...]
    rows[1:2, 0:64] = b1[...]
    rows[2:3, 0:64] = b2[...]
    columns = jnp.transpose(rows[...])
    gain2, bias1, bias2 = columns[0:64, 0:1], columns[0:64, 1:2], columns[0:64, 2:3]
    pl.semaphore_wait(barrier, 5)

    one = Gather(x, z, (x_out, x_in), t1, send1, recv1)
    two = Gather(x, z, (m_out, m_in), t2, send2, recv2)

    def gather(group, make_tile):
        group.start_blocks(OUTER)
        make_tile()
        group.start_tile()
        group.start_blocks(INNER)
        group.relay_tile(0)
        group.relay_blocks(OUTER, 0)
        for k in range(1, 5):
            group.relay_tile(k)
            group.relay_blocks(OUTER, k)
            group.relay_blocks(INNER, k - 1)

    def stats(outer, inner):
        so = jnp.sum(outer * outer, axis=0, keepdims=True)
        si = jnp.sum(inner * inner, axis=0, keepdims=True)
        return so[:, 0:128], si[:, 0:128], si[:, 128:256], so[:, 128:256]

    def put_tile(tiles, outer, inner):
        tiles[z, x] = jnp.zeros((8, 128), F32)
        for i, row in enumerate(stats(outer, inner)):
            tiles[z, x, i : i + 1, :] = row

    def conv_half(half, weights, blocks, scale, gains):
        lo, hi = (0, 3) if half == OUTER else (1, 2)
        row = jnp.concatenate([scale[lo : lo + 1], scale[hi : hi + 1]], axis=1)
        for j in range(16):
            v = blocks[j].astype(F32) * row
            if gains is not None:
                v = v * gains[0:64, j : j + 1]
            act[j * 64 : (j + 1) * 64, :] = silu_of_half(v).astype(BF16)
        y[half] = jnp.dot(weights[...], act[...], preferred_element_type=F32)

    column = lax.rem(lax.broadcasted_iota(jnp.int32, (64, 256), 1), WIDTH)

    def taps(half, q):
        left = y[half, (3 * q) * 64 : (3 * q + 1) * 64, :]
        mid = y[half, (3 * q + 1) * 64 : (3 * q + 2) * 64, :]
        right = y[half, (3 * q + 2) * 64 : (3 * q + 3) * 64, :]
        left = jnp.where(column == 0, 0.0, pltpu.roll(left, 1, 1))
        right = jnp.where(column == WIDTH - 1, 0.0, pltpu.roll(right, 255, 1))
        return left + mid + right

    def halo_copies(phase):
        return [
            pltpu.make_async_remote_copy(
                src_ref=halo_src.at[phase, i],
                dst_ref=halo_dst.at[phase, i],
                send_sem=halo_send.at[phase, i],
                recv_sem=halo_recv.at[phase, i],
                device_id={"rows": row},
                device_id_type=MESH,
            )
            for i, row in enumerate((below, above))
        ]

    def convolve(group, phase, weights, scale, gains):
        group.finish_blocks(OUTER)
        conv_half(OUTER, weights, group.blocks[OUTER], scale, gains)
        down, up = taps(OUTER, 0), taps(OUTER, 2)
        halo_src[phase, 0] = pltpu.roll(down, 64, 1)[:, 0:128]
        halo_src[phase, 1] = pltpu.roll(up, 192, 1)[:, 128:256]
        halos = halo_copies(phase)
        for copy in halos:
            copy.start()
        group.relay_blocks(INNER, 4)
        group.finish_blocks(INNER)
        conv_half(INNER, weights, group.blocks[INNER], scale, gains)

        def full(outer, inner):
            return jnp.concatenate([outer[:, 0:128], inner, outer[:, 128:256]], axis=1)

        down = pltpu.roll(full(down, taps(INNER, 0)), 64, 1)
        up = pltpu.roll(full(up, taps(INNER, 2)), 448, 1)
        mid = full(taps(OUTER, 1), taps(INNER, 1))
        for copy in halos:
            copy.wait_recv()
        lane = lax.broadcasted_iota(jnp.int32, (64, 128), 1)
        from_above = jnp.where(r == 0, 0.0, halo_dst[phase, 0])
        from_below = jnp.where(r == 15, 0.0, halo_dst[phase, 1])
        first = jnp.where(lane < WIDTH, from_above, down[:, 0:128])
        last = jnp.where(lane < WIDTH, up[:, 384:512], from_below)
        down = jnp.concatenate([first, down[:, 128:512]], axis=1)
        up = jnp.concatenate([up[:, 0:384], last], axis=1)
        return mid + down + up, halos

    for load in loads[:3]:
        load.wait()

    def tile_one():
        put_tile(t1, x_out[c].astype(F32), x_in[c].astype(F32))
        t1[z, x, 4:5, 0:64] = g1[...]

    gather(one, tile_one)
    gains = jnp.transpose(
        jnp.concatenate([t1[j % 8, j // 8, 4:5, :] for j in range(16)], axis=0)
    )
    loads[3].wait()
    middle, halos1 = convolve(one, 0, wa, scale_rows(t1[...], 0.5), gains)
    middle = middle + bias1
    scaled = (middle * gain2).astype(BF16)
    m_out[c, :, 0:128] = scaled[:, 0:128]
    m_out[c, :, 128:256] = scaled[:, 384:512]
    m_in[c] = scaled[:, 128:384]

    def tile_two():
        outer = jnp.concatenate([middle[:, 0:128], middle[:, 384:512]], axis=1)
        put_tile(t2, outer, middle[:, 128:384])

    gather(two, tile_two)
    loads[4].wait()
    result, halos2 = convolve(two, 1, wb, scale_rows(t2[...], 0.5), None)
    result = result + bias2
    out[:, 0:128] = (result[:, 0:128] + x_out[c, :, 0:128].astype(F32)).astype(BF16)
    out[:, 128:384] = (result[:, 128:384] + x_in[c].astype(F32)).astype(BF16)
    out[:, 384:512] = (result[:, 384:512] + x_out[c, :, 128:256].astype(F32)).astype(BF16)

    one.wait_sends()
    two.wait_sends()
    for copy in halos1 + halos2:
        copy.wait_send()


def on_device(features, gain_first, weight_first, bias_first, gain_second, weight_second, bias_second):
    anywhere = pl.BlockSpec(memory_space=pl.ANY)
    vmem = pl.BlockSpec(memory_space=pltpu.VMEM)
    items = len(KEYS)
    dma = pltpu.SemaphoreType.DMA
    result = pl.pallas_call(
        kernel,
        name="resblock",
        out_shape=jax.ShapeDtypeStruct((64, 512), BF16),
        in_specs=[anywhere, vmem, anywhere, vmem, vmem, anywhere, vmem],
        out_specs=vmem,
        scratch_shapes=[
            pltpu.VMEM((16, 64, 256), BF16),
            pltpu.VMEM((16, 64, 256), BF16),
            pltpu.VMEM((16, 64, 256), BF16),
            pltpu.VMEM((16, 64, 256), BF16),
            pltpu.VMEM((8, 2, 8, 128), F32),
            pltpu.VMEM((8, 2, 8, 128), F32),
            pltpu.VMEM((1024, 256), BF16),
            pltpu.VMEM((576, 1024), BF16),
            pltpu.VMEM((576, 1024), BF16),
            pltpu.VMEM((2, 576, 256), F32),
            pltpu.VMEM((8, 128), F32),
            pltpu.VMEM((2, 2, 64, 128), F32),
            pltpu.VMEM((2, 2, 64, 128), F32),
            dma((5,)),
            dma((items,)),
            dma((items,)),
            dma((items,)),
            dma((items,)),
            dma((2, 2)),
            dma((2, 2)),
        ],
        compiler_params=pltpu.CompilerParams(collective_id=0, has_side_effects=True),
    )(
        features.reshape(64, 512),
        gain_first.reshape(1, 64),
        weight_first.reshape(27 * 64, 1024),
        bias_first.reshape(1, 64),
        gain_second.reshape(1, 64),
        weight_second.reshape(27 * 64, 1024),
        bias_second.reshape(1, 64),
    )
    return result.reshape(64, 1, 512)


def solution(mesh):
    in_specs = (
        P("chan", None, "rows"),
        P("chan"),
        P(None, None, None, "chan", None),
        P("chan"),
        P("chan"),
        P(None, None, None, "chan", None),
        P("chan"),
    )
    out_specs = P("chan", None, "rows")
    return jax.shard_map(
        on_device, mesh=mesh, in_specs=in_specs, out_specs=out_specs, check_vma=False
    )
```

```python
import jax
import jax.numpy as jnp
from jax import lax
from jax.experimental import pallas as pl
from jax.experimental.pallas import tpu as pltpu
from jax.sharding import PartitionSpec as P

CH = 1024
WIDTH = 64
EPS = 1e-6
F32 = jnp.float32
BF16 = jnp.bfloat16
MESH = pl.DeviceIdType.MESH

GAINS, EDGE, INNER = 0, 1, 2
ITEMS = [(0, dz) for dz in (1, -1, 2, -2, 3, -3, 4)] + [(1, dz) for dz in (0, 1, -1, 2, -2, 3, -3, 4)]
INDEX = {(part, *item): i for i, (part, item) in enumerate((p, t) for p in range(3) for t in ITEMS)}


class Gather:
    def __init__(self, x, z, buffers, send_sem, recv_sem):
        self.x, self.z = x, z
        self.buffers = buffers
        self.send_sem, self.recv_sem = send_sem, recv_sem
        self.sent = []
        self.waited = set()

    def ref(self, part, col, dz):
        column = 1 - self.x if col else self.x
        return self.buffers[part].at[column * 8 + lax.rem(self.z - dz + 8, 8)]

    def copy(self, part, col, dz, key, chan):
        i = INDEX[key]
        ref = self.ref(part, col, dz)
        return pltpu.make_async_remote_copy(
            src_ref=ref,
            dst_ref=ref,
            send_sem=self.send_sem.at[i],
            recv_sem=self.recv_sem.at[i],
            device_id={"chan": chan},
            device_id_type=MESH,
        )

    def send(self, part, col, dz, cross, step):
        chan = (1 - self.x if cross else self.x) * 8 + lax.rem(self.z + step + 8, 8)
        far = 4 if abs(dz + step) == 4 else dz + step
        copy = self.copy(part, col, dz, (part, col ^ cross, far), chan)
        copy.start()
        self.sent.append(copy)

    def wait(self, part, col, dz):
        if (part, col, dz) not in self.waited:
            self.waited.add((part, col, dz))
            self.copy(part, col, dz, (part, col, dz), (1 - self.x) * 8 + self.z).wait_recv()

    def start(self, part):
        for cross, step in ((0, 2), (0, -2), (1, 0), (0, 1), (0, -1)):
            self.send(part, 0, 0, cross, step)

    def from_partner(self, part):
        self.wait(part, 1, 0)
        for step in (1, -1):
            self.send(part, 1, 0, 0, step)

    def from_two_away(self, part):
        far = -1 if part == INNER else 1
        routes = [(sign, 1, 0) for sign in (far, -far)]
        routes += [(far, 1, 2 * far), (far, 1, far), (-far, 1, -far), (far, 0, 2 * far), (far, 0, far), (-far, 0, -far)]
        for sign, cross, step in routes:
            self.wait(part, 0, 2 * sign)
            self.send(part, 0, 2 * sign, cross, step)

    def finish(self, part):
        for col, dz in ITEMS:
            self.wait(part, col, dz)

    def wait_sends(self):
        for copy in self.sent:
            copy.wait_send()


def silu_of_half(h):
    return h * (1.0 + jnp.tanh(h))


def kernel(
    feat, g1, w1, b1, g2, w2, b2, out,
    loaded, x_edge, x_in, m_edge, m_in, gains, act_edge, act_in, wa, wb, y_edge, y_in, rows, halo_src, halo_dst,
    load_sem, send1, recv1, send2, recv2, halo_send, halo_recv,
):
    r, c = lax.axis_index("rows"), lax.axis_index("chan")
    x, z = c // 8, lax.rem(c, 8)
    above, below = lax.rem(r + 15, 16), lax.rem(r + 1, 16)

    loads = [
        pltpu.make_async_copy(feat, loaded, load_sem.at[0]),
        pltpu.make_async_copy(w1.at[pl.ds(18 * 64, 9 * 64)], wa, load_sem.at[1]),
        pltpu.make_async_copy(w2.at[pl.ds(18 * 64, 9 * 64)], wb, load_sem.at[2]),
    ]
    for load in loads:
        load.start()

    barrier = pltpu.get_barrier_semaphore()
    peers = [{"chan": x * 8 + lax.rem(z + step, 8)} for step in (1, 2, 6, 7)]
    peers += [{"chan": (1 - x) * 8 + lax.rem(z + step, 8)} for step in (0, 1, 2, 6, 7)]
    peers += [{"rows": above}, {"rows": below}]
    for peer in peers:
        pl.semaphore_signal(barrier, inc=1, device_id=peer, device_id_type=MESH)
    gains[c] = jnp.zeros((2, 128), F32)
    gains[c, 0:1, 0:64] = g1[...]
    gains[c, 1:2, 0:64] = g2[...]
    rows[...] = jnp.zeros_like(rows)
    rows[0:1, 0:64] = b1[...]
    rows[1:2, 0:64] = b2[...]
    columns = jnp.transpose(rows[...])
    bias1, bias2 = columns[0:64, 0:1], columns[0:64, 1:2]
    lane = lax.broadcasted_iota(jnp.int32, (64, 128), 1)
    half = lane[0:32] < WIDTH

    def beside(left, right):
        return jnp.where(lane < WIDTH, left, right)

    def split(tiles):
        first, second, third, last = tiles
        return beside(first, last), jnp.concatenate([beside(last, first), second, third], axis=1)

    def joined(edge, inner):
        mixed = inner[:, 0:128]
        return jnp.concatenate([beside(edge, mixed), inner[:, 128:384], beside(mixed, edge)], axis=1)

    def place(value, edge, inner):
        edges, inside = split([value[:, 128 * i : 128 * (i + 1)] for i in range(4)])
        edge[c] = edges.astype(BF16)
        inner[c] = inside.astype(BF16)

    loads[0].wait()
    place(loaded[...].astype(F32), x_edge, x_in)
    pl.semaphore_wait(barrier, len(peers))

    one = Gather(x, z, (gains, x_edge, x_in), send1, recv1)
    two = Gather(x, z, (gains, m_edge, m_in), send2, recv2)

    def gather(group, with_gains):
        small = (GAINS,) if with_gains else ()
        for part in (EDGE, *small, INNER):
            group.start(part)
        for part in (EDGE, *small, INNER):
            group.from_partner(part)
            group.from_two_away(part)

    def products(weights, blocks, columns, act, y):
        total = sum(jnp.square(blocks[j].astype(F32)) for j in range(16))
        scale = 0.5 * lax.rsqrt(jnp.sum(total, axis=0, keepdims=True) / CH + EPS)
        for j in range(16):
            v = blocks[j].astype(F32) * scale * columns[0:64, j : j + 1]
            act[j * 64 : (j + 1) * 64, :] = silu_of_half(v).astype(BF16)
        y[...] = jnp.dot(weights[...], act[...], preferred_element_type=F32)

    def taps(y, q):
        width = y.shape[1]
        column = lax.rem(lax.broadcasted_iota(jnp.int32, (64, width), 1), WIDTH)
        left, mid, right = (y[(3 * q + i) * 64 : (3 * q + i + 1) * 64, :] for i in range(3))
        left = jnp.where(column == 0, 0.0, pltpu.roll(left, 1, 1))
        right = jnp.where(column == WIDTH - 1, 0.0, pltpu.roll(right, width - 1, 1))
        return left + mid + right

    def halo_copies(phase):
        return [
            pltpu.make_async_remote_copy(
                src_ref=halo_src.at[phase, i],
                dst_ref=halo_dst.at[phase, i],
                send_sem=halo_send.at[phase, i],
                recv_sem=halo_recv.at[phase, i],
                device_id={"rows": row},
                device_id_type=MESH,
            )
            for i, row in enumerate((below, above))
        ]

    def convolve(group, phase, weights, columns):
        for part in (EDGE, GAINS) if phase == 0 else (EDGE,):
            group.finish(part)
        columns = columns()
        products(weights, group.buffers[EDGE], columns, act_edge, y_edge)
        down, up = taps(y_edge, 0), taps(y_edge, 2)
        halo_src[phase, 0] = jnp.where(half, pltpu.roll(down[0:32], 64, 1), down[32:64])
        halo_src[phase, 1] = jnp.where(half, up[0:32], pltpu.roll(up[32:64], 64, 1))
        halos = halo_copies(phase)
        for copy in halos:
            copy.start()
        mid = taps(y_edge, 1)
        group.finish(INNER)
        products(weights, group.buffers[INNER], columns, act_in, y_in)
        down = pltpu.roll(joined(down, taps(y_in, 0)), 64, 1)
        up = pltpu.roll(joined(up, taps(y_in, 2)), 448, 1)
        mid = joined(mid, taps(y_in, 1))
        for copy in halos:
            copy.wait_recv()
        packed = halo_dst[phase, 0]
        from_above = jnp.where(r == 0, 0.0, jnp.concatenate([packed, pltpu.roll(packed, 64, 1)], axis=0))
        packed = halo_dst[phase, 1]
        from_below = jnp.where(r == 15, 0.0, jnp.concatenate([pltpu.roll(packed, 64, 1), packed], axis=0))
        down = jnp.concatenate([beside(from_above, down[:, 0:128]), down[:, 128:512]], axis=1)
        up = jnp.concatenate([up[:, 0:384], beside(up[:, 384:512], from_below)], axis=1)
        return mid + down + up, halos

    def gain_columns(which):
        return jnp.transpose(jnp.concatenate([gains[j, which : which + 1, :] for j in range(16)], axis=0))

    gather(one, True)
    loads[1].wait()
    middle, halos1 = convolve(one, 0, wa, lambda: gain_columns(0))
    place(middle + bias1, m_edge, m_in)
    gather(two, False)
    loads[2].wait()
    result, halos2 = convolve(two, 1, wb, lambda: gain_columns(1))
    out[...] = (result + bias2 + loaded[...].astype(F32)).astype(BF16)

    one.wait_sends()
    two.wait_sends()
    for copy in halos1 + halos2:
        copy.wait_send()


def on_device(features, gain_first, weight_first, bias_first, gain_second, weight_second, bias_second):
    anywhere = pl.BlockSpec(memory_space=pl.ANY)
    vmem = pl.BlockSpec(memory_space=pltpu.VMEM)
    items = len(INDEX)
    dma = pltpu.SemaphoreType.DMA
    result = pl.pallas_call(
        kernel,
        name="resblock",
        out_shape=jax.ShapeDtypeStruct((64, 512), BF16),
        in_specs=[anywhere, vmem, anywhere, vmem, vmem, anywhere, vmem],
        out_specs=vmem,
        scratch_shapes=[
            pltpu.VMEM((64, 512), BF16),
            pltpu.VMEM((16, 64, 128), BF16),
            pltpu.VMEM((16, 64, 384), BF16),
            pltpu.VMEM((16, 64, 128), BF16),
            pltpu.VMEM((16, 64, 384), BF16),
            pltpu.VMEM((16, 2, 128), F32),
            pltpu.VMEM((1024, 128), BF16),
            pltpu.VMEM((1024, 384), BF16),
            pltpu.VMEM((576, 1024), BF16),
            pltpu.VMEM((576, 1024), BF16),
            pltpu.VMEM((576, 128), F32),
            pltpu.VMEM((576, 384), F32),
            pltpu.VMEM((8, 128), F32),
            pltpu.VMEM((2, 2, 32, 128), F32),
            pltpu.VMEM((2, 2, 32, 128), F32),
            dma((3,)),
            dma((items,)),
            dma((items,)),
            dma((items,)),
            dma((items,)),
            dma((2, 2)),
            dma((2, 2)),
        ],
        compiler_params=pltpu.CompilerParams(collective_id=0, has_side_effects=True),
    )(
        features.reshape(64, 512),
        gain_first.reshape(1, 64),
        weight_first.reshape(27 * 64, 1024),
        bias_first.reshape(1, 64),
        gain_second.reshape(1, 64),
        weight_second.reshape(27 * 64, 1024),
        bias_second.reshape(1, 64),
    )
    return result.reshape(64, 1, 512)


def solution(mesh):
    in_specs = (
        P("chan", None, "rows"),
        P("chan"),
        P(None, None, None, "chan", None),
        P("chan"),
        P("chan"),
        P(None, None, None, "chan", None),
        P("chan"),
    )
    out_specs = P("chan", None, "rows")
    return jax.shard_map(
        on_device, mesh=mesh, in_specs=in_specs, out_specs=out_specs, check_vma=False
    )
```

```python
import jax
import jax.numpy as jnp
from jax import lax
from jax.experimental import pallas as pl
from jax.experimental.pallas import tpu as pltpu
from jax.sharding import PartitionSpec as P

CH = 1024
WIDTH = 64
EPS = 1e-6
F32 = jnp.float32
BF16 = jnp.bfloat16
MESH = pl.DeviceIdType.MESH

GAINS, EDGE, NEXT, INNER = 0, 1, 2, 3
ITEMS = [(0, dz) for dz in (1, -1, 2, -2, 3, -3, 4)] + [(1, dz) for dz in (0, 1, -1, 2, -2, 3, -3, 4)]
INDEX = {(part, *item): i for i, (part, item) in enumerate((p, t) for p in range(4) for t in ITEMS)}


class Gather:
    def __init__(self, x, z, buffers, send_sem, recv_sem):
        self.x, self.z = x, z
        self.buffers = buffers
        self.send_sem, self.recv_sem = send_sem, recv_sem
        self.sent = []
        self.waited = set()

    def ref(self, part, col, dz):
        column = 1 - self.x if col else self.x
        return self.buffers[part].at[column * 8 + lax.rem(self.z - dz + 8, 8)]

    def copy(self, part, col, dz, key, chan):
        i = INDEX[key]
        ref = self.ref(part, col, dz)
        return pltpu.make_async_remote_copy(
            src_ref=ref,
            dst_ref=ref,
            send_sem=self.send_sem.at[i],
            recv_sem=self.recv_sem.at[i],
            device_id={"chan": chan},
            device_id_type=MESH,
        )

    def send(self, part, col, dz, cross, step):
        chan = (1 - self.x if cross else self.x) * 8 + lax.rem(self.z + step + 8, 8)
        far = 4 if abs(dz + step) == 4 else dz + step
        copy = self.copy(part, col, dz, (part, col ^ cross, far), chan)
        copy.start()
        self.sent.append(copy)

    def wait(self, part, col, dz):
        if (part, col, dz) not in self.waited:
            self.waited.add((part, col, dz))
            self.copy(part, col, dz, (part, col, dz), (1 - self.x) * 8 + self.z).wait_recv()

    def start(self, part):
        for cross, step in ((0, 2), (0, -2), (1, 0), (0, 1), (0, -1)):
            self.send(part, 0, 0, cross, step)

    def from_partner(self, part):
        self.wait(part, 1, 0)
        for step in (1, -1):
            self.send(part, 1, 0, 0, step)

    def from_two_away(self, part):
        far = -1 if part == INNER else 1
        routes = [(sign, 1, 0) for sign in (far, -far)]
        routes += [(far, 1, 2 * far), (far, 1, far), (-far, 1, -far), (far, 0, 2 * far), (far, 0, far), (-far, 0, -far)]
        for sign, cross, step in routes:
            self.wait(part, 0, 2 * sign)
            self.send(part, 0, 2 * sign, cross, step)

    def finish(self, part):
        for col, dz in ITEMS:
            self.wait(part, col, dz)

    def wait_sends(self):
        for copy in self.sent:
            copy.wait_send()


def silu_of_half(h):
    return h * (1.0 + jnp.tanh(h))


def kernel(
    feat, g1, w1, b1, g2, w2, b2, out,
    loaded, x_edge, x_next, x_in, m_edge, m_next, m_in, gains,
    act_edge, act_next, act_in, wa, wb, y_edge, y_next, y_in, rows, halo_src, halo_dst,
    small, load_sem, send1, recv1, send2, recv2, halo_send, halo_recv,
):
    r, c = lax.axis_index("rows"), lax.axis_index("chan")
    x, z = c // 8, lax.rem(c, 8)
    above, below = lax.rem(r + 15, 16), lax.rem(r + 1, 16)

    loads = [
        pltpu.make_async_copy(feat, loaded, load_sem.at[0]),
        pltpu.make_async_copy(w1.at[pl.ds(18 * 64, 9 * 64)], wa, load_sem.at[1]),
        pltpu.make_async_copy(w2.at[pl.ds(18 * 64, 9 * 64)], wb, load_sem.at[2]),
    ]
    smalls = [
        pltpu.make_async_copy(ref, small.at[i], load_sem.at[3 + i])
        for i, ref in enumerate((g1, g2, b1, b2))
    ]
    for load in smalls + loads:
        load.start()

    barrier = pltpu.get_barrier_semaphore()
    peers = [{"chan": x * 8 + lax.rem(z + step, 8)} for step in (1, 2, 6, 7)]
    peers += [{"chan": (1 - x) * 8 + z}, {"rows": above}, {"rows": below}]
    for peer in peers:
        pl.semaphore_signal(barrier, inc=1, device_id=peer, device_id_type=MESH)
    for load in smalls:
        load.wait()
    gains[c] = jnp.zeros((2, 128), F32)
    gains[c, 0:1, 0:64] = small[0]
    gains[c, 1:2, 0:64] = small[1]
    rows[...] = jnp.zeros_like(rows)
    rows[0:1, 0:64] = small[2]
    rows[1:2, 0:64] = small[3]
    columns = jnp.transpose(rows[...])
    bias1, bias2 = columns[0:64, 0:1], columns[0:64, 1:2]
    lane = lax.broadcasted_iota(jnp.int32, (64, 128), 1)
    column = lax.rem(lane, WIDTH)

    def beside(left, right):
        return jnp.where(lane[0 : left.shape[0]] < WIDTH, left, right)

    def swapped(tile):
        return pltpu.roll(tile, 64, 1)

    def place(tiles, edge, following, inner):
        edge[c] = tiles[0].astype(BF16)
        following[c] = tiles[1].astype(BF16)
        inner[c, :, 0:128] = tiles[2].astype(BF16)
        inner[c, :, 128:256] = tiles[3].astype(BF16)

    loads[0].wait()
    natural = [loaded[:, 128 * i : 128 * (i + 1)].astype(F32) for i in range(4)]
    place(
        [
            beside(natural[0], natural[3]),
            swapped(beside(natural[3], natural[0])),
            beside(natural[1], natural[2]),
            swapped(beside(natural[2], natural[1])),
        ],
        x_edge, x_next, x_in,
    )
    pl.semaphore_wait(barrier, len(peers))

    one = Gather(x, z, (gains, x_edge, x_next, x_in), send1, recv1)
    two = Gather(x, z, (gains, m_edge, m_next, m_in), send2, recv2)

    def gather(group, with_gains):
        parts = (EDGE, GAINS, NEXT, INNER) if with_gains else (EDGE, NEXT, INNER)
        for part in parts:
            group.start(part)
        for part in parts:
            group.from_partner(part)
            group.from_two_away(part)

    def activate(group, part, columns, act):
        blocks = group.buffers[part]
        total = jnp.square(blocks[c].astype(F32))
        for col, dz in ITEMS:
            group.wait(part, col, dz)
            source = (1 - x if col else x) * 8 + lax.rem(z - dz + 8, 8)
            total = total + jnp.square(blocks[source].astype(F32))
        scale = 0.5 * lax.rsqrt(jnp.sum(total, axis=0, keepdims=True) / CH + EPS)
        for j in range(16):
            v = blocks[j].astype(F32) * scale * columns[0:64, j : j + 1]
            act[j * 64 : (j + 1) * 64, :] = silu_of_half(v).astype(BF16)

    def multiply(weights, act, y, top, count):
        y[top : top + count, :] = jnp.dot(
            weights[top : top + count, :], act[...], preferred_element_type=F32
        )

    def tile(t, q, s):
        ref = (y_edge, y_next, y_in, y_in)[t]
        at = (3 * q + s) * 64
        return ref[at : at + 64, 128:256] if t == 3 else ref[at : at + 64, 0:128]

    def over_columns(left, mid, right):
        left = jnp.where(column == 0, 0.0, pltpu.roll(left, 1, 1))
        right = jnp.where(column == WIDTH - 1, 0.0, pltpu.roll(right, 127, 1))
        return mid + left + right

    def over_rows(t, s):
        if t == 0:
            return tile(0, 1, s) + beside(tile(1, 2, s), tile(1, 0, s))
        if t == 3:
            turned = swapped(beside(tile(3, 0, s), tile(3, 2, s)))
            return tile(3, 1, s) + turned + beside(tile(2, 0, s), tile(2, 2, s))
        return tile(t, 1, s) + beside(
            tile(t - 1, 0, s) + tile(t + 1, 2, s), tile(t + 1, 0, s) + tile(t - 1, 2, s)
        )

    def halo_copies(phase):
        return [
            pltpu.make_async_remote_copy(
                src_ref=halo_src.at[phase, i],
                dst_ref=halo_dst.at[phase, i],
                send_sem=halo_send.at[phase, i],
                recv_sem=halo_recv.at[phase, i],
                device_id={"rows": row},
                device_id_type=MESH,
            )
            for i, row in enumerate((below, above))
        ]

    def convolve(group, phase, weights, columns):
        activate(group, EDGE, columns, act_edge)
        multiply(weights, act_edge, y_edge, 0, 192)
        multiply(weights, act_edge, y_edge, 384, 192)
        down = over_columns(*(tile(0, 0, s) for s in range(3)))
        up = over_columns(*(tile(0, 2, s) for s in range(3)))
        halo_src[phase, 0] = beside(swapped(down[0:32]), down[32:64])
        halo_src[phase, 1] = beside(up[0:32], swapped(up[32:64]))
        halos = halo_copies(phase)
        for copy in halos:
            copy.start()
        multiply(weights, act_edge, y_edge, 192, 192)
        activate(group, NEXT, columns, act_next)
        multiply(weights, act_next, y_next, 0, 288)
        multiply(weights, act_next, y_next, 288, 288)
        activate(group, INNER, columns, act_in)
        multiply(weights, act_in, y_in, 0, 288)
        multiply(weights, act_in, y_in, 288, 288)
        tiles = [over_columns(*(over_rows(t, s) for s in range(3))) for t in range(4)]
        for copy in halos:
            copy.wait_recv()
        packed = halo_dst[phase, 0]
        from_above = jnp.where(r == 0, 0.0, jnp.concatenate([packed, swapped(packed)], axis=0))
        packed = halo_dst[phase, 1]
        from_below = jnp.where(r == 15, 0.0, jnp.concatenate([swapped(packed), packed], axis=0))
        tiles[0] = tiles[0] + beside(from_above, from_below)
        return tiles, halos

    def gain_columns(which):
        return jnp.transpose(jnp.concatenate([gains[j, which : which + 1, :] for j in range(16)], axis=0))

    gather(one, True)
    loads[1].wait()
    one.finish(GAINS)
    gain1, gain2 = gain_columns(0), gain_columns(1)
    middle, halos1 = convolve(one, 0, wa, gain1)
    place([part + bias1 for part in middle], m_edge, m_next, m_in)
    gather(two, False)
    loads[2].wait()
    result, halos2 = convolve(two, 1, wb, gain2)
    second, last = swapped(result[1]), swapped(result[3])
    ordered = [beside(result[0], second), beside(result[2], last), beside(last, result[2]), beside(second, result[0])]
    for i, part in enumerate(ordered):
        lanes = slice(128 * i, 128 * (i + 1))
        out[:, lanes] = (part + bias2 + loaded[:, lanes].astype(F32)).astype(BF16)

    one.wait_sends()
    two.wait_sends()
    for copy in halos1 + halos2:
        copy.wait_send()


def on_device(features, gain_first, weight_first, bias_first, gain_second, weight_second, bias_second):
    anywhere = pl.BlockSpec(memory_space=pl.ANY)
    vmem = pl.BlockSpec(memory_space=pltpu.VMEM)
    items = len(INDEX)
    dma = pltpu.SemaphoreType.DMA
    result = pl.pallas_call(
        kernel,
        name="resblock",
        out_shape=jax.ShapeDtypeStruct((64, 512), BF16),
        in_specs=[anywhere] * 7,
        out_specs=vmem,
        scratch_shapes=[
            pltpu.VMEM((64, 512), BF16),
            pltpu.VMEM((16, 64, 128), BF16),
            pltpu.VMEM((16, 64, 128), BF16),
            pltpu.VMEM((16, 64, 256), BF16),
            pltpu.VMEM((16, 64, 128), BF16),
            pltpu.VMEM((16, 64, 128), BF16),
            pltpu.VMEM((16, 64, 256), BF16),
            pltpu.VMEM((16, 2, 128), F32),
            pltpu.VMEM((1024, 128), BF16),
            pltpu.VMEM((1024, 128), BF16),
            pltpu.VMEM((1024, 256), BF16),
            pltpu.VMEM((576, 1024), BF16),
            pltpu.VMEM((576, 1024), BF16),
            pltpu.VMEM((576, 128), F32),
            pltpu.VMEM((576, 128), F32),
            pltpu.VMEM((576, 256), F32),
            pltpu.VMEM((8, 128), F32),
            pltpu.VMEM((2, 2, 32, 128), F32),
            pltpu.VMEM((2, 2, 32, 128), F32),
            pltpu.VMEM((4, 1, 64), F32),
            dma((7,)),
            dma((items,)),
            dma((items,)),
            dma((items,)),
            dma((items,)),
            dma((2, 2)),
            dma((2, 2)),
        ],
        compiler_params=pltpu.CompilerParams(collective_id=0, has_side_effects=True),
    )(
        features.reshape(64, 512),
        gain_first.reshape(1, 64),
        weight_first.reshape(27 * 64, 1024),
        bias_first.reshape(1, 64),
        gain_second.reshape(1, 64),
        weight_second.reshape(27 * 64, 1024),
        bias_second.reshape(1, 64),
    )
    return result.reshape(64, 1, 512)


def solution(mesh):
    in_specs = (
        P("chan", None, "rows"),
        P("chan"),
        P(None, None, None, "chan", None),
        P("chan"),
        P("chan"),
        P(None, None, None, "chan", None),
        P("chan"),
    )
    out_specs = P("chan", None, "rows")
    return jax.shard_map(
        on_device, mesh=mesh, in_specs=in_specs, out_specs=out_specs, check_vma=False
    )
```

```python
import jax
import jax.numpy as jnp
from jax import lax
from jax.experimental import pallas as pl
from jax.experimental.pallas import tpu as pltpu
from jax.sharding import PartitionSpec as P

CH = 1024
WIDTH = 64
EPS = 1e-6
F32 = jnp.float32
BF16 = jnp.bfloat16
MESH = pl.DeviceIdType.MESH

GAINS, EDGE, NEXT, INNER = 0, 1, 2, 3
ITEMS = [(0, dz) for dz in (1, -1, 2, -2, 3, -3, 4)] + [(1, dz) for dz in (0, 1, -1, 2, -2, 3, -3, 4)]
INDEX = {(part, *item): i for i, (part, item) in enumerate((p, t) for p in range(4) for t in ITEMS)}


class Gather:
    def __init__(self, x, z, buffers, send_sem, recv_sem):
        self.x, self.z = x, z
        self.buffers = buffers
        self.send_sem, self.recv_sem = send_sem, recv_sem
        self.sent = []
        self.waited = set()

    def ref(self, part, col, dz):
        column = 1 - self.x if col else self.x
        return self.buffers[part].at[column * 8 + lax.rem(self.z - dz + 8, 8)]

    def copy(self, part, col, dz, key, chan):
        i = INDEX[key]
        ref = self.ref(part, col, dz)
        return pltpu.make_async_remote_copy(
            src_ref=ref,
            dst_ref=ref,
            send_sem=self.send_sem.at[i],
            recv_sem=self.recv_sem.at[i],
            device_id={"chan": chan},
            device_id_type=MESH,
        )

    def send(self, part, col, dz, cross, step):
        chan = (1 - self.x if cross else self.x) * 8 + lax.rem(self.z + step + 8, 8)
        far = 4 if abs(dz + step) == 4 else dz + step
        copy = self.copy(part, col, dz, (part, col ^ cross, far), chan)
        copy.start()
        self.sent.append(copy)

    def wait(self, part, col, dz):
        if (part, col, dz) not in self.waited:
            self.waited.add((part, col, dz))
            self.copy(part, col, dz, (part, col, dz), (1 - self.x) * 8 + self.z).wait_recv()

    def start(self, part):
        for cross, step in ((0, 2), (0, -2), (1, 0)):
            self.send(part, 0, 0, cross, step)

    def near(self, part):
        for step in (1, -1):
            self.send(part, 0, 0, 0, step)

    def from_partner(self, part):
        self.wait(part, 1, 0)
        for step in (1, -1):
            self.send(part, 1, 0, 0, step)

    def from_two_away(self, part):
        far = -1 if part == INNER else 1
        routes = [(sign, 1, 0) for sign in (far, -far)]
        routes += [(far, 1, 2 * far), (far, 1, far), (-far, 1, -far), (far, 0, 2 * far), (far, 0, far), (-far, 0, -far)]
        for sign, cross, step in routes:
            self.wait(part, 0, 2 * sign)
            self.send(part, 0, 2 * sign, cross, step)

    def finish(self, part):
        for col, dz in ITEMS:
            self.wait(part, col, dz)

    def wait_sends(self):
        for copy in self.sent:
            copy.wait_send()


def silu_of_half(h):
    return h * (1.0 + jnp.tanh(h))


def kernel(
    feat, g1, w1, b1, g2, w2, b2, out,
    loaded, x_edge, x_next, x_in, m_edge, m_next, m_in, gains,
    act_edge, act_next, act_in, wa, wb, y_edge, y_next, y_in, rows, halo_src, halo_dst,
    small, load_sem, send1, recv1, send2, recv2, halo_send, halo_recv,
):
    r, c = lax.axis_index("rows"), lax.axis_index("chan")
    x, z = c // 8, lax.rem(c, 8)
    above, below = lax.rem(r + 15, 16), lax.rem(r + 1, 16)

    loads = [
        pltpu.make_async_copy(feat, loaded, load_sem.at[0]),
        pltpu.make_async_copy(w1.at[pl.ds(18 * 64, 9 * 64)], wa, load_sem.at[1]),
        pltpu.make_async_copy(w2.at[pl.ds(18 * 64, 9 * 64)], wb, load_sem.at[2]),
    ]
    smalls = [
        pltpu.make_async_copy(ref, small.at[i], load_sem.at[3 + i])
        for i, ref in enumerate((g1, g2, b1, b2))
    ]
    for load in smalls + loads:
        load.start()

    barrier = pltpu.get_barrier_semaphore()
    peers = [{"chan": x * 8 + lax.rem(z + step, 8)} for step in (1, 2, 6, 7)]
    peers += [{"chan": (1 - x) * 8 + z}, {"rows": above}, {"rows": below}]
    for peer in peers:
        pl.semaphore_signal(barrier, inc=1, device_id=peer, device_id_type=MESH)
    for load in smalls:
        load.wait()
    gains[c] = jnp.zeros((2, 128), F32)
    gains[c, 0:1, 0:64] = small[0]
    gains[c, 1:2, 0:64] = small[1]
    rows[...] = jnp.zeros_like(rows)
    rows[0:1, 0:64] = small[2]
    rows[1:2, 0:64] = small[3]
    columns = jnp.transpose(rows[...])
    bias1, bias2 = columns[0:64, 0:1], columns[0:64, 1:2]
    lane = lax.broadcasted_iota(jnp.int32, (64, 128), 1)
    column = lax.rem(lane, WIDTH)

    def beside(left, right):
        return jnp.where(lane[0 : left.shape[0]] < WIDTH, left, right)

    def swapped(tile):
        return pltpu.roll(tile, 64, 1)

    def place(tiles, edge, following, inner):
        edge[c] = tiles[0].astype(BF16)
        following[c] = tiles[1].astype(BF16)
        inner[c, :, 0:128] = tiles[2].astype(BF16)
        inner[c, :, 128:256] = tiles[3].astype(BF16)

    loads[0].wait()
    natural = [loaded[:, 128 * i : 128 * (i + 1)].astype(F32) for i in range(4)]
    place(
        [
            beside(natural[0], natural[3]),
            swapped(beside(natural[3], natural[0])),
            beside(natural[1], natural[2]),
            swapped(beside(natural[2], natural[1])),
        ],
        x_edge, x_next, x_in,
    )
    pl.semaphore_wait(barrier, len(peers))

    one = Gather(x, z, (gains, x_edge, x_next, x_in), send1, recv1)
    two = Gather(x, z, (gains, m_edge, m_next, m_in), send2, recv2)

    def gather(group, with_gains):
        parts = (EDGE, GAINS, NEXT, INNER) if with_gains else (EDGE, NEXT, INNER)
        for part in parts:
            group.start(part)
            if part != INNER:
                group.near(part)
        for part in parts:
            group.from_partner(part)
            group.from_two_away(part)
        group.near(INNER)

    def activate(group, part, columns, act):
        blocks = group.buffers[part]
        total = jnp.square(blocks[c].astype(F32))
        for col, dz in ITEMS:
            group.wait(part, col, dz)
            source = (1 - x if col else x) * 8 + lax.rem(z - dz + 8, 8)
            total = total + jnp.square(blocks[source].astype(F32))
        scale = 0.5 * lax.rsqrt(jnp.sum(total, axis=0, keepdims=True) / CH + EPS)
        for j in range(16):
            v = blocks[j].astype(F32) * scale * columns[0:64, j : j + 1]
            act[j * 64 : (j + 1) * 64, :] = silu_of_half(v).astype(BF16)

    def multiply(weights, act, y, top, count):
        y[top : top + count, :] = jnp.dot(
            weights[top : top + count, :], act[...], preferred_element_type=F32
        )

    def tile(t, q, s):
        ref = (y_edge, y_next, y_in, y_in)[t]
        at = (3 * q + s) * 64
        return ref[at : at + 64, 128:256] if t == 3 else ref[at : at + 64, 0:128]

    def over_columns(left, mid, right):
        left = jnp.where(column == 0, 0.0, pltpu.roll(left, 1, 1))
        right = jnp.where(column == WIDTH - 1, 0.0, pltpu.roll(right, 127, 1))
        return mid + left + right

    def over_rows(t, s):
        if t == 0:
            return tile(0, 1, s) + beside(tile(1, 2, s), tile(1, 0, s))
        if t == 3:
            turned = swapped(beside(tile(3, 0, s), tile(3, 2, s)))
            return tile(3, 1, s) + turned + beside(tile(2, 0, s), tile(2, 2, s))
        return tile(t, 1, s) + beside(
            tile(t - 1, 0, s) + tile(t + 1, 2, s), tile(t + 1, 0, s) + tile(t - 1, 2, s)
        )

    def halo_copies(phase):
        return [
            pltpu.make_async_remote_copy(
                src_ref=halo_src.at[phase, i],
                dst_ref=halo_dst.at[phase, i],
                send_sem=halo_send.at[phase, i],
                recv_sem=halo_recv.at[phase, i],
                device_id={"rows": row},
                device_id_type=MESH,
            )
            for i, row in enumerate((below, above))
        ]

    def convolve(group, phase, weights, columns):
        activate(group, EDGE, columns, act_edge)
        multiply(weights, act_edge, y_edge, 0, 192)
        multiply(weights, act_edge, y_edge, 384, 192)
        down = over_columns(*(tile(0, 0, s) for s in range(3)))
        up = over_columns(*(tile(0, 2, s) for s in range(3)))
        halo_src[phase, 0] = beside(swapped(down[0:32]), down[32:64])
        halo_src[phase, 1] = beside(up[0:32], swapped(up[32:64]))
        halos = halo_copies(phase)
        for copy in halos:
            copy.start()
        multiply(weights, act_edge, y_edge, 192, 192)
        activate(group, NEXT, columns, act_next)
        multiply(weights, act_next, y_next, 0, 288)
        multiply(weights, act_next, y_next, 288, 288)
        activate(group, INNER, columns, act_in)
        multiply(weights, act_in, y_in, 0, 288)
        multiply(weights, act_in, y_in, 288, 288)
        tiles = [over_columns(*(over_rows(t, s) for s in range(3))) for t in range(4)]
        for copy in halos:
            copy.wait_recv()
        packed = halo_dst[phase, 0]
        from_above = jnp.where(r == 0, 0.0, jnp.concatenate([packed, swapped(packed)], axis=0))
        packed = halo_dst[phase, 1]
        from_below = jnp.where(r == 15, 0.0, jnp.concatenate([swapped(packed), packed], axis=0))
        tiles[0] = tiles[0] + beside(from_above, from_below)
        return tiles, halos

    def gain_columns(which):
        return jnp.transpose(jnp.concatenate([gains[j, which : which + 1, :] for j in range(16)], axis=0))

    gather(one, True)
    loads[1].wait()
    one.finish(GAINS)
    gain1, gain2 = gain_columns(0), gain_columns(1)
    middle, halos1 = convolve(one, 0, wa, gain1)
    place([part + bias1 for part in middle], m_edge, m_next, m_in)
    gather(two, False)
    loads[2].wait()
    result, halos2 = convolve(two, 1, wb, gain2)
    second, last = swapped(result[1]), swapped(result[3])
    ordered = [beside(result[0], second), beside(result[2], last), beside(last, result[2]), beside(second, result[0])]
    for i, part in enumerate(ordered):
        lanes = slice(128 * i, 128 * (i + 1))
        out[:, lanes] = (part + bias2 + loaded[:, lanes].astype(F32)).astype(BF16)

    one.wait_sends()
    two.wait_sends()
    for copy in halos1 + halos2:
        copy.wait_send()


def on_device(features, gain_first, weight_first, bias_first, gain_second, weight_second, bias_second):
    anywhere = pl.BlockSpec(memory_space=pl.ANY)
    vmem = pl.BlockSpec(memory_space=pltpu.VMEM)
    items = len(INDEX)
    dma = pltpu.SemaphoreType.DMA
    result = pl.pallas_call(
        kernel,
        name="resblock",
        out_shape=jax.ShapeDtypeStruct((64, 512), BF16),
        in_specs=[anywhere] * 7,
        out_specs=vmem,
        scratch_shapes=[
            pltpu.VMEM((64, 512), BF16),
            pltpu.VMEM((16, 64, 128), BF16),
            pltpu.VMEM((16, 64, 128), BF16),
            pltpu.VMEM((16, 64, 256), BF16),
            pltpu.VMEM((16, 64, 128), BF16),
            pltpu.VMEM((16, 64, 128), BF16),
            pltpu.VMEM((16, 64, 256), BF16),
            pltpu.VMEM((16, 2, 128), F32),
            pltpu.VMEM((1024, 128), BF16),
            pltpu.VMEM((1024, 128), BF16),
            pltpu.VMEM((1024, 256), BF16),
            pltpu.VMEM((576, 1024), BF16),
            pltpu.VMEM((576, 1024), BF16),
            pltpu.VMEM((576, 128), F32),
            pltpu.VMEM((576, 128), F32),
            pltpu.VMEM((576, 256), F32),
            pltpu.VMEM((8, 128), F32),
            pltpu.VMEM((2, 2, 32, 128), F32),
            pltpu.VMEM((2, 2, 32, 128), F32),
            pltpu.VMEM((4, 1, 64), F32),
            dma((7,)),
            dma((items,)),
            dma((items,)),
            dma((items,)),
            dma((items,)),
            dma((2, 2)),
            dma((2, 2)),
        ],
        compiler_params=pltpu.CompilerParams(collective_id=0, has_side_effects=True),
    )(
        features.reshape(64, 512),
        gain_first.reshape(1, 64),
        weight_first.reshape(27 * 64, 1024),
        bias_first.reshape(1, 64),
        gain_second.reshape(1, 64),
        weight_second.reshape(27 * 64, 1024),
        bias_second.reshape(1, 64),
    )
    return result.reshape(64, 1, 512)


def solution(mesh):
    in_specs = (
        P("chan", None, "rows"),
        P("chan"),
        P(None, None, None, "chan", None),
        P("chan"),
        P("chan"),
        P(None, None, None, "chan", None),
        P("chan"),
    )
    out_specs = P("chan", None, "rows")
    return jax.shard_map(
        on_device, mesh=mesh, in_specs=in_specs, out_specs=out_specs, check_vma=False
    )
```

```python
import jax
import jax.numpy as jnp
from jax import lax
from jax.experimental import pallas as pl
from jax.experimental.pallas import tpu as pltpu
from jax.sharding import PartitionSpec as P

CH = 1024
WIDTH = 64
EPS = 1e-6
F32 = jnp.float32
BF16 = jnp.bfloat16
MESH = pl.DeviceIdType.MESH

GAINS, EDGE, NEXT, INNER = 0, 1, 2, 3
ITEMS = [(0, dz) for dz in (1, -1, 2, -2, 3, -3, 4)] + [(1, dz) for dz in (0, 1, -1, 2, -2, 3, -3, 4)]
INDEX = {(part, *item): i for i, (part, item) in enumerate((p, t) for p in range(4) for t in ITEMS)}


class Gather:
    def __init__(self, x, z, buffers, send_sem, recv_sem):
        self.x, self.z = x, z
        self.buffers = buffers
        self.send_sem, self.recv_sem = send_sem, recv_sem
        self.sent = []
        self.waited = set()

    def ref(self, part, col, dz):
        column = 1 - self.x if col else self.x
        return self.buffers[part].at[column * 8 + lax.rem(self.z - dz + 8, 8)]

    def copy(self, part, col, dz, key, chan):
        i = INDEX[key]
        ref = self.ref(part, col, dz)
        return pltpu.make_async_remote_copy(
            src_ref=ref,
            dst_ref=ref,
            send_sem=self.send_sem.at[i],
            recv_sem=self.recv_sem.at[i],
            device_id={"chan": chan},
            device_id_type=MESH,
        )

    def send(self, part, col, dz, cross, step):
        chan = (1 - self.x if cross else self.x) * 8 + lax.rem(self.z + step + 8, 8)
        far = 4 if abs(dz + step) == 4 else dz + step
        copy = self.copy(part, col, dz, (part, col ^ cross, far), chan)
        copy.start()
        self.sent.append(copy)

    def wait(self, part, col, dz):
        if (part, col, dz) not in self.waited:
            self.waited.add((part, col, dz))
            self.copy(part, col, dz, (part, col, dz), (1 - self.x) * 8 + self.z).wait_recv()

    def start(self, part):
        for cross, step in ((0, 2), (0, -2), (1, 0)):
            self.send(part, 0, 0, cross, step)

    def near(self, part):
        for step in (1, -1):
            self.send(part, 0, 0, 0, step)

    def from_partner(self, part):
        self.wait(part, 1, 0)
        for step in (1, -1):
            self.send(part, 1, 0, 0, step)

    def from_two_away(self, part):
        far = -1 if part == INNER else 1
        routes = [(sign, 1, 0) for sign in (far, -far)]
        routes += [(far, 1, 2 * far), (far, 1, far), (-far, 1, -far), (far, 0, 2 * far), (far, 0, far), (-far, 0, -far)]
        for sign, cross, step in routes:
            self.wait(part, 0, 2 * sign)
            self.send(part, 0, 2 * sign, cross, step)

    def finish(self, part):
        for col, dz in ITEMS:
            self.wait(part, col, dz)

    def wait_sends(self):
        for copy in self.sent:
            copy.wait_send()


def silu_of_half(h):
    return h * (1.0 + jnp.tanh(h))


def packed(v):
    square = v * v
    return v * square * (square * square)


def unpacked(power):
    size = jnp.exp(jnp.log(jnp.maximum(jnp.abs(power), 1e-37)) * (1.0 / 7.0))
    return jnp.where(power < 0.0, -size, jnp.where(power > 0.0, size, 0.0))


def kernel(
    feat, g1, w1, b1, g2, w2, b2, out,
    loaded, x_edge, x_next, x_in, m_edge, m_next, m_in, gains,
    act_edge, act_next, act_in, wa, wb, y_edge, y_next, y_in, plain_edge, plain_next, plain_in, rows, halo_src, halo_dst,
    small, load_sem, send1, recv1, send2, recv2, halo_send, halo_recv,
):
    r, c = lax.axis_index("rows"), lax.axis_index("chan")
    x, z = c // 8, lax.rem(c, 8)
    above, below = lax.rem(r + 15, 16), lax.rem(r + 1, 16)

    loads = [
        pltpu.make_async_copy(feat, loaded, load_sem.at[0]),
        pltpu.make_async_copy(w1.at[pl.ds(18 * 64, 9 * 64)], wa, load_sem.at[1]),
        pltpu.make_async_copy(w2.at[pl.ds(18 * 64, 9 * 64)], wb, load_sem.at[2]),
    ]
    smalls = [
        pltpu.make_async_copy(ref, small.at[i], load_sem.at[3 + i])
        for i, ref in enumerate((g1, g2, b1, b2))
    ]
    for load in smalls + loads:
        load.start()

    barrier = pltpu.get_barrier_semaphore()
    peers = [{"chan": x * 8 + lax.rem(z + step, 8)} for step in (1, 2, 6, 7)]
    peers += [{"chan": (1 - x) * 8 + z}, {"rows": above}, {"rows": below}]
    for peer in peers:
        pl.semaphore_signal(barrier, inc=1, device_id=peer, device_id_type=MESH)
    for load in smalls:
        load.wait()
    gains[c] = jnp.zeros((2, 128), F32)
    gains[c, 0:1, 0:64] = small[0]
    gains[c, 1:2, 0:64] = small[1]
    rows[...] = jnp.zeros_like(rows)
    rows[0:1, 0:64] = small[2]
    rows[1:2, 0:64] = small[3]
    columns = jnp.transpose(rows[...])
    bias1, bias2 = columns[0:64, 0:1], columns[0:64, 1:2]
    lane = lax.broadcasted_iota(jnp.int32, (64, 128), 1)
    column = lax.rem(lane, WIDTH)

    def beside(left, right):
        return jnp.where(lane[0 : left.shape[0]] < WIDTH, left, right)

    def swapped(tile):
        return pltpu.roll(tile, 64, 1)

    def place(tiles, edge, following, inner):
        edge[c] = tiles[0].astype(BF16)
        following[c] = tiles[1].astype(BF16)
        inner[c, :, 0:128] = tiles[2].astype(BF16)
        inner[c, :, 128:256] = tiles[3].astype(BF16)

    loads[0].wait()
    natural = [loaded[:, 128 * i : 128 * (i + 1)].astype(F32) for i in range(4)]
    place(
        [
            beside(natural[0], natural[3]),
            swapped(beside(natural[3], natural[0])),
            beside(natural[1], natural[2]),
            swapped(beside(natural[2], natural[1])),
        ],
        x_edge, x_next, x_in,
    )
    pl.semaphore_wait(barrier, len(peers))

    one = Gather(x, z, (gains, x_edge, x_next, x_in), send1, recv1)
    two = Gather(x, z, (gains, m_edge, m_next, m_in), send2, recv2)

    def gather(group, with_gains):
        parts = (EDGE, GAINS, NEXT, INNER) if with_gains else (EDGE, NEXT, INNER)
        for part in parts:
            group.start(part)
            if part != INNER:
                group.near(part)
        for part in parts:
            group.from_partner(part)
            group.from_two_away(part)
        group.near(INNER)

    def activate(group, part, columns, act, plain):
        blocks = group.buffers[part]

        def value(source):
            v = blocks[source].astype(F32)
            if group is one:
                return v
            v = unpacked(v)
            plain[source] = v
            return v

        total = jnp.square(value(c))
        for col, dz in ITEMS:
            group.wait(part, col, dz)
            source = (1 - x if col else x) * 8 + lax.rem(z - dz + 8, 8)
            total = total + jnp.square(value(source))
        scale = 0.5 * lax.rsqrt(jnp.sum(total, axis=0, keepdims=True) / CH + EPS)
        for j in range(16):
            v = blocks[j].astype(F32) if group is one else plain[j]
            act[j * 64 : (j + 1) * 64, :] = silu_of_half(v * scale * columns[0:64, j : j + 1]).astype(BF16)

    def multiply(weights, act, y, top, count):
        y[top : top + count, :] = jnp.dot(
            weights[top : top + count, :], act[...], preferred_element_type=F32
        )

    def tile(t, q, s):
        ref = (y_edge, y_next, y_in, y_in)[t]
        at = (3 * q + s) * 64
        return ref[at : at + 64, 128:256] if t == 3 else ref[at : at + 64, 0:128]

    def over_columns(left, mid, right):
        left = jnp.where(column == 0, 0.0, pltpu.roll(left, 1, 1))
        right = jnp.where(column == WIDTH - 1, 0.0, pltpu.roll(right, 127, 1))
        return mid + left + right

    def over_rows(t, s):
        if t == 0:
            return tile(0, 1, s) + beside(tile(1, 2, s), tile(1, 0, s))
        if t == 3:
            turned = swapped(beside(tile(3, 0, s), tile(3, 2, s)))
            return tile(3, 1, s) + turned + beside(tile(2, 0, s), tile(2, 2, s))
        return tile(t, 1, s) + beside(
            tile(t - 1, 0, s) + tile(t + 1, 2, s), tile(t + 1, 0, s) + tile(t - 1, 2, s)
        )

    def halo_copies(phase):
        return [
            pltpu.make_async_remote_copy(
                src_ref=halo_src.at[phase, i],
                dst_ref=halo_dst.at[phase, i],
                send_sem=halo_send.at[phase, i],
                recv_sem=halo_recv.at[phase, i],
                device_id={"rows": row},
                device_id_type=MESH,
            )
            for i, row in enumerate((below, above))
        ]

    def convolve(group, phase, weights, columns):
        activate(group, EDGE, columns, act_edge, plain_edge)
        multiply(weights, act_edge, y_edge, 0, 192)
        multiply(weights, act_edge, y_edge, 384, 192)
        down = over_columns(*(tile(0, 0, s) for s in range(3)))
        up = over_columns(*(tile(0, 2, s) for s in range(3)))
        halo_src[phase, 0] = beside(swapped(down[0:32]), down[32:64])
        halo_src[phase, 1] = beside(up[0:32], swapped(up[32:64]))
        halos = halo_copies(phase)
        for copy in halos:
            copy.start()
        multiply(weights, act_edge, y_edge, 192, 192)
        activate(group, NEXT, columns, act_next, plain_next)
        multiply(weights, act_next, y_next, 0, 288)
        multiply(weights, act_next, y_next, 288, 288)
        activate(group, INNER, columns, act_in, plain_in)
        multiply(weights, act_in, y_in, 0, 288)
        multiply(weights, act_in, y_in, 288, 288)
        tiles = [over_columns(*(over_rows(t, s) for s in range(3))) for t in range(4)]
        for copy in halos:
            copy.wait_recv()
        pair = halo_dst[phase, 0]
        from_above = jnp.where(r == 0, 0.0, jnp.concatenate([pair, swapped(pair)], axis=0))
        pair = halo_dst[phase, 1]
        from_below = jnp.where(r == 15, 0.0, jnp.concatenate([swapped(pair), pair], axis=0))
        tiles[0] = tiles[0] + beside(from_above, from_below)
        return tiles, halos

    def gain_columns(which):
        return jnp.transpose(jnp.concatenate([gains[j, which : which + 1, :] for j in range(16)], axis=0))

    gather(one, True)
    loads[1].wait()
    one.finish(GAINS)
    gain1, gain2 = gain_columns(0), gain_columns(1)
    middle, halos1 = convolve(one, 0, wa, gain1)
    place([packed(part + bias1) for part in middle], m_edge, m_next, m_in)
    gather(two, False)
    loads[2].wait()
    result, halos2 = convolve(two, 1, wb, gain2)
    second, last = swapped(result[1]), swapped(result[3])
    ordered = [beside(result[0], second), beside(result[2], last), beside(last, result[2]), beside(second, result[0])]
    for i, part in enumerate(ordered):
        lanes = slice(128 * i, 128 * (i + 1))
        out[:, lanes] = (part + bias2 + loaded[:, lanes].astype(F32)).astype(BF16)

    one.wait_sends()
    two.wait_sends()
    for copy in halos1 + halos2:
        copy.wait_send()


def on_device(features, gain_first, weight_first, bias_first, gain_second, weight_second, bias_second):
    anywhere = pl.BlockSpec(memory_space=pl.ANY)
    vmem = pl.BlockSpec(memory_space=pltpu.VMEM)
    items = len(INDEX)
    dma = pltpu.SemaphoreType.DMA
    result = pl.pallas_call(
        kernel,
        name="resblock",
        out_shape=jax.ShapeDtypeStruct((64, 512), BF16),
        in_specs=[anywhere] * 7,
        out_specs=vmem,
        scratch_shapes=[
            pltpu.VMEM((64, 512), BF16),
            pltpu.VMEM((16, 64, 128), BF16),
            pltpu.VMEM((16, 64, 128), BF16),
            pltpu.VMEM((16, 64, 256), BF16),
            pltpu.VMEM((16, 64, 128), BF16),
            pltpu.VMEM((16, 64, 128), BF16),
            pltpu.VMEM((16, 64, 256), BF16),
            pltpu.VMEM((16, 2, 128), F32),
            pltpu.VMEM((1024, 128), BF16),
            pltpu.VMEM((1024, 128), BF16),
            pltpu.VMEM((1024, 256), BF16),
            pltpu.VMEM((576, 1024), BF16),
            pltpu.VMEM((576, 1024), BF16),
            pltpu.VMEM((576, 128), F32),
            pltpu.VMEM((576, 128), F32),
            pltpu.VMEM((576, 256), F32),
            pltpu.VMEM((16, 64, 128), F32),
            pltpu.VMEM((16, 64, 128), F32),
            pltpu.VMEM((16, 64, 256), F32),
            pltpu.VMEM((8, 128), F32),
            pltpu.VMEM((2, 2, 32, 128), F32),
            pltpu.VMEM((2, 2, 32, 128), F32),
            pltpu.VMEM((4, 1, 64), F32),
            dma((7,)),
            dma((items,)),
            dma((items,)),
            dma((items,)),
            dma((items,)),
            dma((2, 2)),
            dma((2, 2)),
        ],
        compiler_params=pltpu.CompilerParams(collective_id=0, has_side_effects=True),
    )(
        features.reshape(64, 512),
        gain_first.reshape(1, 64),
        weight_first.reshape(27 * 64, 1024),
        bias_first.reshape(1, 64),
        gain_second.reshape(1, 64),
        weight_second.reshape(27 * 64, 1024),
        bias_second.reshape(1, 64),
    )
    return result.reshape(64, 1, 512)


def solution(mesh):
    in_specs = (
        P("chan", None, "rows"),
        P("chan"),
        P(None, None, None, "chan", None),
        P("chan"),
        P("chan"),
        P(None, None, None, "chan", None),
        P("chan"),
    )
    out_specs = P("chan", None, "rows")
    return jax.shard_map(
        on_device, mesh=mesh, in_specs=in_specs, out_specs=out_specs, check_vma=False
    )
```

```python
import jax
import jax.numpy as jnp
from jax import lax
from jax.experimental import pallas as pl
from jax.experimental.pallas import tpu as pltpu
from jax.sharding import PartitionSpec as P

CH = 1024
WIDTH = 64
EPS = 1e-6
F32 = jnp.float32
BF16 = jnp.bfloat16
MESH = pl.DeviceIdType.MESH

GAINS, EDGE, NEXT, INNER = 0, 1, 2, 3
ITEMS = [(0, dz) for dz in (1, -1, 2, -2, 3, -3, 4)] + [(1, dz) for dz in (0, 1, -1, 2, -2, 3, -3, 4)]
INDEX = {(part, *item): i for i, (part, item) in enumerate((p, t) for p in range(4) for t in ITEMS)}


class Gather:
    def __init__(self, x, z, buffers, send_sem, recv_sem):
        self.x, self.z = x, z
        self.buffers = buffers
        self.send_sem, self.recv_sem = send_sem, recv_sem
        self.sent = []
        self.waited = set()

    def ref(self, part, col, dz):
        column = 1 - self.x if col else self.x
        return self.buffers[part].at[column * 8 + lax.rem(self.z - dz + 8, 8)]

    def copy(self, part, col, dz, key, chan):
        i = INDEX[key]
        ref = self.ref(part, col, dz)
        return pltpu.make_async_remote_copy(
            src_ref=ref,
            dst_ref=ref,
            send_sem=self.send_sem.at[i],
            recv_sem=self.recv_sem.at[i],
            device_id={"chan": chan},
            device_id_type=MESH,
        )

    def send(self, part, col, dz, cross, step):
        chan = (1 - self.x if cross else self.x) * 8 + lax.rem(self.z + step + 8, 8)
        far = 4 if abs(dz + step) == 4 else dz + step
        copy = self.copy(part, col, dz, (part, col ^ cross, far), chan)
        copy.start()
        self.sent.append((part, copy))

    def wait(self, part, col, dz):
        if (part, col, dz) not in self.waited:
            self.waited.add((part, col, dz))
            self.copy(part, col, dz, (part, col, dz), (1 - self.x) * 8 + self.z).wait_recv()

    def start(self, part):
        for cross, step in ((0, 2), (0, -2), (1, 0)):
            self.send(part, 0, 0, cross, step)

    def near(self, part):
        for step in (1, -1):
            self.send(part, 0, 0, 0, step)

    def from_partner(self, part):
        self.wait(part, 1, 0)
        for step in (1, -1):
            self.send(part, 1, 0, 0, step)

    def from_two_away(self, part):
        far = -1 if part == INNER else 1
        routes = [(sign, 1, 0) for sign in (far, -far)]
        routes += [(far, 1, 2 * far), (far, 1, far), (-far, 1, -far), (far, 0, 2 * far), (far, 0, far), (-far, 0, -far)]
        for sign, cross, step in routes:
            self.wait(part, 0, 2 * sign)
            self.send(part, 0, 2 * sign, cross, step)

    def finish(self, part):
        for col, dz in ITEMS:
            self.wait(part, col, dz)

    def wait_sends(self, parts):
        for part, copy in self.sent:
            if part in parts:
                copy.wait_send()


def silu_of_half(h):
    return h * (1.0 + jnp.tanh(h))


def packed(v):
    square = v * v
    return v * square * (square * square)


def unpacked(power):
    size = jnp.exp(jnp.log(jnp.maximum(jnp.abs(power), 1e-37)) * (1.0 / 7.0))
    return jnp.where(power < 0.0, -size, jnp.where(power > 0.0, size, 0.0))


def kernel(
    feat, g1, w1, b1, g2, w2, b2, out,
    loaded, x_edge, x_next, x_in, m_edge, m_next, m_in, gains,
    act_edge, act_next, act_in, wa, wb, y_edge, y_next, y_in, plain_edge, plain_next, plain_in, rows, halo_src, halo_dst,
    small, load_sem, send1, recv1, send2, recv2, halo_send, halo_recv,
):
    r, c = lax.axis_index("rows"), lax.axis_index("chan")
    x, z = c // 8, lax.rem(c, 8)
    above, below = lax.rem(r + 15, 16), lax.rem(r + 1, 16)

    loads = [
        pltpu.make_async_copy(feat, loaded, load_sem.at[0]),
        pltpu.make_async_copy(w1.at[pl.ds(18 * 64, 9 * 64)], wa, load_sem.at[1]),
        pltpu.make_async_copy(w2.at[pl.ds(18 * 64, 9 * 64)], wb, load_sem.at[2]),
    ]
    smalls = [
        pltpu.make_async_copy(ref, small.at[i], load_sem.at[3 + i])
        for i, ref in enumerate((g1, g2, b1, b2))
    ]
    for load in smalls + loads:
        load.start()

    barrier = pltpu.get_barrier_semaphore()
    peers = [{"chan": x * 8 + lax.rem(z + step, 8)} for step in (1, 2, 6, 7)]
    peers += [{"chan": (1 - x) * 8 + z}, {"rows": above}, {"rows": below}]
    for peer in peers:
        pl.semaphore_signal(barrier, inc=1, device_id=peer, device_id_type=MESH)
    for load in smalls:
        load.wait()
    gains[c] = jnp.zeros((2, 128), F32)
    gains[c, 0:1, 0:64] = small[0]
    gains[c, 1:2, 0:64] = small[1]
    rows[...] = jnp.zeros_like(rows)
    rows[0:1, 0:64] = small[2]
    rows[1:2, 0:64] = small[3]
    columns = jnp.transpose(rows[...])
    bias1, bias2 = columns[0:64, 0:1], columns[0:64, 1:2]
    lane = lax.broadcasted_iota(jnp.int32, (64, 128), 1)
    column = lax.rem(lane, WIDTH)

    def beside(left, right):
        return jnp.where(lane[0 : left.shape[0]] < WIDTH, left, right)

    def swapped(tile):
        return pltpu.roll(tile, 64, 1)

    def place(tiles, edge, following, inner):
        edge[c] = tiles[0].astype(BF16)
        following[c] = tiles[1].astype(BF16)
        inner[c, :, 0:128] = tiles[2].astype(BF16)
        inner[c, :, 128:256] = tiles[3].astype(BF16)

    loads[0].wait()
    natural = [loaded[:, 128 * i : 128 * (i + 1)].astype(F32) for i in range(4)]
    place(
        [
            beside(natural[0], natural[3]),
            swapped(beside(natural[3], natural[0])),
            beside(natural[1], natural[2]),
            swapped(beside(natural[2], natural[1])),
        ],
        x_edge, x_next, x_in,
    )
    pl.semaphore_wait(barrier, len(peers))

    one = Gather(x, z, (gains, x_edge, x_next, x_in), send1, recv1)
    two = Gather(x, z, (gains, m_edge, m_next, m_in), send2, recv2)

    def gather(group, with_gains):
        parts = (EDGE, GAINS, NEXT, INNER) if with_gains else (EDGE, NEXT, INNER)
        for part in parts:
            group.start(part)
            if part != INNER:
                group.near(part)
        for part in parts:
            group.from_partner(part)
            group.from_two_away(part)
        group.near(INNER)

    def activate(group, part, columns, act, plain):
        blocks = group.buffers[part]

        def value(source):
            v = blocks[source].astype(F32)
            if group is one:
                return v
            v = unpacked(v)
            plain[source] = v
            return v

        total = jnp.square(value(c))
        for col, dz in ITEMS:
            group.wait(part, col, dz)
            source = (1 - x if col else x) * 8 + lax.rem(z - dz + 8, 8)
            total = total + jnp.square(value(source))
        scale = 0.5 * lax.rsqrt(jnp.sum(total, axis=0, keepdims=True) / CH + EPS)
        for j in range(16):
            v = blocks[j].astype(F32) if group is one else plain[j]
            act[j * 64 : (j + 1) * 64, :] = silu_of_half(v * scale * columns[0:64, j : j + 1]).astype(BF16)

    def multiply(weights, act, y, top, count):
        y[top : top + count, :] = jnp.dot(
            weights[top : top + count, :], act[...], preferred_element_type=F32
        )

    def tile(t, q, s):
        ref = (y_edge, y_next, y_in, y_in)[t]
        at = (3 * q + s) * 64
        return ref[at : at + 64, 128:256] if t == 3 else ref[at : at + 64, 0:128]

    def over_columns(left, mid, right):
        left = jnp.where(column == 0, 0.0, pltpu.roll(left, 1, 1))
        right = jnp.where(column == WIDTH - 1, 0.0, pltpu.roll(right, 127, 1))
        return mid + left + right

    def over_rows(t, s):
        if t == 0:
            return tile(0, 1, s) + beside(tile(1, 2, s), tile(1, 0, s))
        if t == 3:
            turned = swapped(beside(tile(3, 0, s), tile(3, 2, s)))
            return tile(3, 1, s) + turned + beside(tile(2, 0, s), tile(2, 2, s))
        return tile(t, 1, s) + beside(
            tile(t - 1, 0, s) + tile(t + 1, 2, s), tile(t + 1, 0, s) + tile(t - 1, 2, s)
        )

    def halo_copies(phase):
        return [
            pltpu.make_async_remote_copy(
                src_ref=halo_src.at[phase, i],
                dst_ref=halo_dst.at[phase, i],
                send_sem=halo_send.at[phase, i],
                recv_sem=halo_recv.at[phase, i],
                device_id={"rows": row},
                device_id_type=MESH,
            )
            for i, row in enumerate((below, above))
        ]

    def convolve(group, phase, weights, columns):
        activate(group, EDGE, columns, act_edge, plain_edge)
        multiply(weights, act_edge, y_edge, 0, 192)
        multiply(weights, act_edge, y_edge, 384, 192)
        down = over_columns(*(tile(0, 0, s) for s in range(3)))
        up = over_columns(*(tile(0, 2, s) for s in range(3)))
        halo_src[phase, 0] = beside(swapped(down[0:32]), down[32:64])
        halo_src[phase, 1] = beside(up[0:32], swapped(up[32:64]))
        halos = halo_copies(phase)
        for copy in halos:
            copy.start()
        multiply(weights, act_edge, y_edge, 192, 192)
        activate(group, NEXT, columns, act_next, plain_next)
        multiply(weights, act_next, y_next, 0, 288)
        multiply(weights, act_next, y_next, 288, 288)
        group.wait_sends((EDGE, GAINS, NEXT))
        activate(group, INNER, columns, act_in, plain_in)
        multiply(weights, act_in, y_in, 0, 288)
        multiply(weights, act_in, y_in, 288, 288)
        tiles = [over_columns(*(over_rows(t, s) for s in range(3))) for t in range(4)]
        for copy in halos:
            copy.wait_recv()
        pair = halo_dst[phase, 0]
        from_above = jnp.where(r == 0, 0.0, jnp.concatenate([pair, swapped(pair)], axis=0))
        pair = halo_dst[phase, 1]
        from_below = jnp.where(r == 15, 0.0, jnp.concatenate([swapped(pair), pair], axis=0))
        tiles[0] = tiles[0] + beside(from_above, from_below)
        return tiles, halos

    def gain_columns(which):
        return jnp.transpose(jnp.concatenate([gains[j, which : which + 1, :] for j in range(16)], axis=0))

    gather(one, True)
    loads[1].wait()
    one.finish(GAINS)
    gain1, gain2 = gain_columns(0), gain_columns(1)
    middle, halos1 = convolve(one, 0, wa, gain1)
    place([packed(part + bias1) for part in middle], m_edge, m_next, m_in)
    gather(two, False)
    one.wait_sends((INNER,))
    for copy in halos1:
        copy.wait_send()
    loads[2].wait()
    result, halos2 = convolve(two, 1, wb, gain2)
    second, last = swapped(result[1]), swapped(result[3])
    ordered = [beside(result[0], second), beside(result[2], last), beside(last, result[2]), beside(second, result[0])]
    for i, part in enumerate(ordered):
        lanes = slice(128 * i, 128 * (i + 1))
        out[:, lanes] = (part + bias2 + loaded[:, lanes].astype(F32)).astype(BF16)

    two.wait_sends((INNER,))
    for copy in halos2:
        copy.wait_send()


def on_device(features, gain_first, weight_first, bias_first, gain_second, weight_second, bias_second):
    anywhere = pl.BlockSpec(memory_space=pl.ANY)
    vmem = pl.BlockSpec(memory_space=pltpu.VMEM)
    items = len(INDEX)
    dma = pltpu.SemaphoreType.DMA
    result = pl.pallas_call(
        kernel,
        name="resblock",
        out_shape=jax.ShapeDtypeStruct((64, 512), BF16),
        in_specs=[anywhere] * 7,
        out_specs=vmem,
        scratch_shapes=[
            pltpu.VMEM((64, 512), BF16),
            pltpu.VMEM((16, 64, 128), BF16),
            pltpu.VMEM((16, 64, 128), BF16),
            pltpu.VMEM((16, 64, 256), BF16),
            pltpu.VMEM((16, 64, 128), BF16),
            pltpu.VMEM((16, 64, 128), BF16),
            pltpu.VMEM((16, 64, 256), BF16),
            pltpu.VMEM((16, 2, 128), F32),
            pltpu.VMEM((1024, 128), BF16),
            pltpu.VMEM((1024, 128), BF16),
            pltpu.VMEM((1024, 256), BF16),
            pltpu.VMEM((576, 1024), BF16),
            pltpu.VMEM((576, 1024), BF16),
            pltpu.VMEM((576, 128), F32),
            pltpu.VMEM((576, 128), F32),
            pltpu.VMEM((576, 256), F32),
            pltpu.VMEM((16, 64, 128), F32),
            pltpu.VMEM((16, 64, 128), F32),
            pltpu.VMEM((16, 64, 256), F32),
            pltpu.VMEM((8, 128), F32),
            pltpu.VMEM((2, 2, 32, 128), F32),
            pltpu.VMEM((2, 2, 32, 128), F32),
            pltpu.VMEM((4, 1, 64), F32),
            dma((7,)),
            dma((items,)),
            dma((items,)),
            dma((items,)),
            dma((items,)),
            dma((2, 2)),
            dma((2, 2)),
        ],
        compiler_params=pltpu.CompilerParams(collective_id=0, has_side_effects=True),
    )(
        features.reshape(64, 512),
        gain_first.reshape(1, 64),
        weight_first.reshape(27 * 64, 1024),
        bias_first.reshape(1, 64),
        gain_second.reshape(1, 64),
        weight_second.reshape(27 * 64, 1024),
        bias_second.reshape(1, 64),
    )
    return result.reshape(64, 1, 512)


def solution(mesh):
    in_specs = (
        P("chan", None, "rows"),
        P("chan"),
        P(None, None, None, "chan", None),
        P("chan"),
        P("chan"),
        P(None, None, None, "chan", None),
        P("chan"),
    )
    out_specs = P("chan", None, "rows")
    return jax.shard_map(
        on_device, mesh=mesh, in_specs=in_specs, out_specs=out_specs, check_vma=False
    )
```

```python
import jax
import jax.numpy as jnp
from jax import lax
from jax.experimental import pallas as pl
from jax.experimental.pallas import tpu as pltpu
from jax.sharding import PartitionSpec as P

CH = 1024
WIDTH = 64
EPS = 1e-6
F32 = jnp.float32
BF16 = jnp.bfloat16
MESH = pl.DeviceIdType.MESH

GAINS, EDGE, NEXT, INNER = 0, 1, 2, 3
ITEMS = [(0, dz) for dz in (1, -1, 2, -2, 3, -3, 4)] + [(1, dz) for dz in (0, 1, -1, 2, -2, 3, -3, 4)]
INDEX = {(part, *item): i for i, (part, item) in enumerate((p, t) for p in range(4) for t in ITEMS)}


class Gather:
    def __init__(self, x, z, buffers, send_sem, recv_sem):
        self.x, self.z = x, z
        self.buffers = buffers
        self.send_sem, self.recv_sem = send_sem, recv_sem
        self.sent = []
        self.waited = set()

    def ref(self, part, col, dz):
        column = 1 - self.x if col else self.x
        return self.buffers[part].at[column * 8 + lax.rem(self.z - dz + 8, 8)]

    def copy(self, part, col, dz, key, chan):
        i = INDEX[key]
        ref = self.ref(part, col, dz)
        return pltpu.make_async_remote_copy(
            src_ref=ref,
            dst_ref=ref,
            send_sem=self.send_sem.at[i],
            recv_sem=self.recv_sem.at[i],
            device_id={"chan": chan},
            device_id_type=MESH,
        )

    def send(self, part, col, dz, cross, step):
        chan = (1 - self.x if cross else self.x) * 8 + lax.rem(self.z + step + 8, 8)
        far = 4 if abs(dz + step) == 4 else dz + step
        copy = self.copy(part, col, dz, (part, col ^ cross, far), chan)
        copy.start()
        self.sent.append((part, copy))

    def wait(self, part, col, dz):
        if (part, col, dz) not in self.waited:
            self.waited.add((part, col, dz))
            self.copy(part, col, dz, (part, col, dz), (1 - self.x) * 8 + self.z).wait_recv()

    def start(self, part):
        for cross, step in ((1, 0), (0, 2), (0, -2)):
            self.send(part, 0, 0, cross, step)

    def near(self, part):
        for step in (1, -1):
            self.send(part, 0, 0, 0, step)

    def from_partner(self, part):
        self.wait(part, 1, 0)
        for step in (1, -1):
            self.send(part, 1, 0, 0, step)

    def from_two_away(self, part):
        far = -1 if part == INNER else 1
        routes = [(sign, 1, 0) for sign in (far, -far)]
        routes += [(far, 1, 2 * far), (far, 1, far), (-far, 1, -far), (far, 0, 2 * far), (far, 0, far), (-far, 0, -far)]
        for sign, cross, step in routes:
            self.wait(part, 0, 2 * sign)
            self.send(part, 0, 2 * sign, cross, step)

    def finish(self, part):
        for col, dz in ITEMS:
            self.wait(part, col, dz)

    def wait_sends(self, parts):
        for part, copy in self.sent:
            if part in parts:
                copy.wait_send()


def silu_of_half(h):
    return h * (1.0 + jnp.tanh(h))


def packed(v):
    square = v * v
    return v * square * (square * square)


def unpacked(power):
    size = jnp.exp(jnp.log(jnp.maximum(jnp.abs(power), 1e-37)) * (1.0 / 7.0))
    return jnp.where(power < 0.0, -size, jnp.where(power > 0.0, size, 0.0))


def kernel(
    feat, g1, w1, b1, g2, w2, b2, out,
    loaded, x_edge, x_next, x_in, m_edge, m_next, m_in, gains,
    act_edge, act_next, act_in, wa, wb, y_edge, y_next, y_in, plain_edge, plain_next, plain_in, rows, halo_src, halo_dst,
    small, load_sem, send1, recv1, send2, recv2, halo_send, halo_recv,
):
    r, c = lax.axis_index("rows"), lax.axis_index("chan")
    x, z = c // 8, lax.rem(c, 8)
    above, below = lax.rem(r + 15, 16), lax.rem(r + 1, 16)

    loads = [
        pltpu.make_async_copy(feat, loaded, load_sem.at[0]),
        pltpu.make_async_copy(w1.at[pl.ds(18 * 64, 9 * 64)], wa, load_sem.at[1]),
        pltpu.make_async_copy(w2.at[pl.ds(18 * 64, 9 * 64)], wb, load_sem.at[2]),
    ]
    smalls = [
        pltpu.make_async_copy(ref, small.at[i], load_sem.at[3 + i])
        for i, ref in enumerate((g1, g2, b1, b2))
    ]
    for load in smalls + loads:
        load.start()

    barrier = pltpu.get_barrier_semaphore()
    peers = [{"chan": x * 8 + lax.rem(z + step, 8)} for step in (1, 2, 6, 7)]
    peers += [{"chan": (1 - x) * 8 + z}, {"rows": above}, {"rows": below}]
    for peer in peers:
        pl.semaphore_signal(barrier, inc=1, device_id=peer, device_id_type=MESH)
    for load in smalls:
        load.wait()
    gains[c] = jnp.zeros((2, 128), F32)
    gains[c, 0:1, 0:64] = small[0]
    gains[c, 1:2, 0:64] = small[1]
    rows[...] = jnp.zeros_like(rows)
    rows[0:1, 0:64] = small[2]
    rows[1:2, 0:64] = small[3]
    columns = jnp.transpose(rows[...])
    bias1, bias2 = columns[0:64, 0:1], columns[0:64, 1:2]
    lane = lax.broadcasted_iota(jnp.int32, (64, 128), 1)
    column = lax.rem(lane, WIDTH)

    def beside(left, right):
        return jnp.where(lane[0 : left.shape[0]] < WIDTH, left, right)

    def swapped(tile):
        return pltpu.roll(tile, 64, 1)

    def place(tiles, edge, following, inner):
        edge[c] = tiles[0].astype(BF16)
        following[c] = tiles[1].astype(BF16)
        inner[c, :, 0:128] = tiles[2].astype(BF16)
        inner[c, :, 128:256] = tiles[3].astype(BF16)

    loads[0].wait()
    natural = [loaded[:, 128 * i : 128 * (i + 1)].astype(F32) for i in range(4)]
    place(
        [
            beside(natural[0], natural[3]),
            swapped(beside(natural[3], natural[0])),
            beside(natural[1], natural[2]),
            swapped(beside(natural[2], natural[1])),
        ],
        x_edge, x_next, x_in,
    )
    pl.semaphore_wait(barrier, len(peers))

    one = Gather(x, z, (gains, x_edge, x_next, x_in), send1, recv1)
    two = Gather(x, z, (gains, m_edge, m_next, m_in), send2, recv2)

    def gather(group, with_gains):
        parts = (EDGE, GAINS, NEXT, INNER) if with_gains else (EDGE, NEXT, INNER)
        for part in parts:
            group.start(part)
            if part != INNER:
                group.near(part)
        for part in parts:
            group.from_partner(part)
            group.from_two_away(part)
        group.near(INNER)

    def activate(group, part, columns, act, plain):
        blocks = group.buffers[part]

        def value(source):
            v = blocks[source].astype(F32)
            if group is one:
                return v
            v = unpacked(v)
            plain[source] = v
            return v

        total = jnp.square(value(c))
        for col, dz in ITEMS:
            group.wait(part, col, dz)
            source = (1 - x if col else x) * 8 + lax.rem(z - dz + 8, 8)
            total = total + jnp.square(value(source))
        scale = 0.5 * lax.rsqrt(jnp.sum(total, axis=0, keepdims=True) / CH + EPS)
        for j in range(16):
            v = blocks[j].astype(F32) if group is one else plain[j]
            act[j * 64 : (j + 1) * 64, :] = silu_of_half(v * scale * columns[0:64, j : j + 1]).astype(BF16)

    def multiply(weights, act, y, top, count):
        y[top : top + count, :] = jnp.dot(
            weights[top : top + count, :], act[...], preferred_element_type=F32
        )

    def tile(t, q, s):
        ref = (y_edge, y_next, y_in, y_in)[t]
        at = (3 * q + s) * 64
        return ref[at : at + 64, 128:256] if t == 3 else ref[at : at + 64, 0:128]

    def over_columns(left, mid, right):
        left = jnp.where(column == 0, 0.0, pltpu.roll(left, 1, 1))
        right = jnp.where(column == WIDTH - 1, 0.0, pltpu.roll(right, 127, 1))
        return mid + left + right

    def over_rows(t, s):
        if t == 0:
            return tile(0, 1, s) + beside(tile(1, 2, s), tile(1, 0, s))
        if t == 3:
            turned = swapped(beside(tile(3, 0, s), tile(3, 2, s)))
            return tile(3, 1, s) + turned + beside(tile(2, 0, s), tile(2, 2, s))
        return tile(t, 1, s) + beside(
            tile(t - 1, 0, s) + tile(t + 1, 2, s), tile(t + 1, 0, s) + tile(t - 1, 2, s)
        )

    def halo_copies(phase):
        return [
            pltpu.make_async_remote_copy(
                src_ref=halo_src.at[phase, i],
                dst_ref=halo_dst.at[phase, i],
                send_sem=halo_send.at[phase, i],
                recv_sem=halo_recv.at[phase, i],
                device_id={"rows": row},
                device_id_type=MESH,
            )
            for i, row in enumerate((below, above))
        ]

    def convolve(group, phase, weights, columns):
        activate(group, EDGE, columns, act_edge, plain_edge)
        multiply(weights, act_edge, y_edge, 0, 192)
        multiply(weights, act_edge, y_edge, 384, 192)
        down = over_columns(*(tile(0, 0, s) for s in range(3)))
        up = over_columns(*(tile(0, 2, s) for s in range(3)))
        halo_src[phase, 0] = beside(swapped(down[0:32]), down[32:64])
        halo_src[phase, 1] = beside(up[0:32], swapped(up[32:64]))
        halos = halo_copies(phase)
        for copy in halos:
            copy.start()
        multiply(weights, act_edge, y_edge, 192, 192)
        activate(group, NEXT, columns, act_next, plain_next)
        multiply(weights, act_next, y_next, 0, 288)
        multiply(weights, act_next, y_next, 288, 288)
        group.wait_sends((EDGE, GAINS, NEXT))
        activate(group, INNER, columns, act_in, plain_in)
        multiply(weights, act_in, y_in, 0, 288)
        multiply(weights, act_in, y_in, 288, 288)
        tiles = [over_columns(*(over_rows(t, s) for s in range(3))) for t in range(4)]
        for copy in halos:
            copy.wait_recv()
        pair = halo_dst[phase, 0]
        from_above = jnp.where(r == 0, 0.0, jnp.concatenate([pair, swapped(pair)], axis=0))
        pair = halo_dst[phase, 1]
        from_below = jnp.where(r == 15, 0.0, jnp.concatenate([swapped(pair), pair], axis=0))
        tiles[0] = tiles[0] + beside(from_above, from_below)
        return tiles, halos

    def gain_columns(which):
        return jnp.transpose(jnp.concatenate([gains[j, which : which + 1, :] for j in range(16)], axis=0))

    gather(one, True)
    loads[1].wait()
    one.finish(GAINS)
    gain1, gain2 = gain_columns(0), gain_columns(1)
    middle, halos1 = convolve(one, 0, wa, gain1)
    place([packed(part + bias1) for part in middle], m_edge, m_next, m_in)
    gather(two, False)
    one.wait_sends((INNER,))
    for copy in halos1:
        copy.wait_send()
    loads[2].wait()
    result, halos2 = convolve(two, 1, wb, gain2)
    second, last = swapped(result[1]), swapped(result[3])
    ordered = [beside(result[0], second), beside(result[2], last), beside(last, result[2]), beside(second, result[0])]
    for i, part in enumerate(ordered):
        lanes = slice(128 * i, 128 * (i + 1))
        out[:, lanes] = (part + bias2 + loaded[:, lanes].astype(F32)).astype(BF16)

    two.wait_sends((INNER,))
    for copy in halos2:
        copy.wait_send()


def on_device(features, gain_first, weight_first, bias_first, gain_second, weight_second, bias_second):
    anywhere = pl.BlockSpec(memory_space=pl.ANY)
    vmem = pl.BlockSpec(memory_space=pltpu.VMEM)
    items = len(INDEX)
    dma = pltpu.SemaphoreType.DMA
    result = pl.pallas_call(
        kernel,
        name="resblock",
        out_shape=jax.ShapeDtypeStruct((64, 512), BF16),
        in_specs=[anywhere] * 7,
        out_specs=vmem,
        scratch_shapes=[
            pltpu.VMEM((64, 512), BF16),
            pltpu.VMEM((16, 64, 128), BF16),
            pltpu.VMEM((16, 64, 128), BF16),
            pltpu.VMEM((16, 64, 256), BF16),
            pltpu.VMEM((16, 64, 128), BF16),
            pltpu.VMEM((16, 64, 128), BF16),
            pltpu.VMEM((16, 64, 256), BF16),
            pltpu.VMEM((16, 2, 128), F32),
            pltpu.VMEM((1024, 128), BF16),
            pltpu.VMEM((1024, 128), BF16),
            pltpu.VMEM((1024, 256), BF16),
            pltpu.VMEM((576, 1024), BF16),
            pltpu.VMEM((576, 1024), BF16),
            pltpu.VMEM((576, 128), F32),
            pltpu.VMEM((576, 128), F32),
            pltpu.VMEM((576, 256), F32),
            pltpu.VMEM((16, 64, 128), F32),
            pltpu.VMEM((16, 64, 128), F32),
            pltpu.VMEM((16, 64, 256), F32),
            pltpu.VMEM((8, 128), F32),
            pltpu.VMEM((2, 2, 32, 128), F32),
            pltpu.VMEM((2, 2, 32, 128), F32),
            pltpu.VMEM((4, 1, 64), F32),
            dma((7,)),
            dma((items,)),
            dma((items,)),
            dma((items,)),
            dma((items,)),
            dma((2, 2)),
            dma((2, 2)),
        ],
        compiler_params=pltpu.CompilerParams(collective_id=0, has_side_effects=True),
    )(
        features.reshape(64, 512),
        gain_first.reshape(1, 64),
        weight_first.reshape(27 * 64, 1024),
        bias_first.reshape(1, 64),
        gain_second.reshape(1, 64),
        weight_second.reshape(27 * 64, 1024),
        bias_second.reshape(1, 64),
    )
    return result.reshape(64, 1, 512)


def solution(mesh):
    in_specs = (
        P("chan", None, "rows"),
        P("chan"),
        P(None, None, None, "chan", None),
        P("chan"),
        P("chan"),
        P(None, None, None, "chan", None),
        P("chan"),
    )
    out_specs = P("chan", None, "rows")
    return jax.shard_map(
        on_device, mesh=mesh, in_specs=in_specs, out_specs=out_specs, check_vma=False
    )
```
